32 devices in a mesh: ctx: 8 (over y, x, core), head: 4 (over z).
Axes of the slice: x: 2, y: 2, z: 4, core: 2. Of those that a mesh axis runs over, the one named last changes fastest.
Arguments:
- light_query: bfloat16 [16384, 2048], P(('ctx', 'head')), may hold values from -6 to 6
- light_key: bfloat16 [16384, 2048], P(('ctx', 'head')), may hold values from -6 to 6
- light_value: bfloat16 [16384, 2048], P(('ctx', 'head')), may hold values from -6 to 6
- soft_query: bfloat16 [16384, 2048], P(('ctx', 'head')), may hold values from -52 to 52
- soft_key: bfloat16 [16384, 2048], P(('ctx', 'head')), may hold values from -6 to 6
- upstream: bfloat16 [16384, 2048], P(('ctx', 'head')), may hold values from -6 to 6
- decays: bfloat16 [16384, 32], P(('ctx', 'head')), may hold values from 0 to 1
- block_mask: int32 [128, 16], P('ctx'), may hold values from 0 to 1, as said below
Outputs:
- grad_light_query: bfloat16 [16384, 2048], P(('ctx', 'head'))
- grad_light_key: bfloat16 [16384, 2048], P(('ctx', 'head'))
- grad_light_value: bfloat16 [16384, 2048], P(('ctx', 'head'))
The draws below stay inside these ranges and needn't reach their ends.
Inputs may be any that keep to these rules, and one draw needn't show every extreme that they name: `block_mask`: in each query block, the flag of its own block within the span is 1 and flags of later blocks are 0; earlier blocks are 0 or 1.
All inputs are finite; a program needn't handle non-finite values.
Results may differ from the reference program's by a relative error of at most 0.0057.
Values may be sent and summed in bfloat16 or wider, within the bound.
No kernel may reach another device: no remote copies, remote signals or barrier semaphores. Data moves between devices by JAX's collectives and lax.ppermute only.
A program may use at most 128 MiB of HBM per device.

```python
import math
import jax
import jax.numpy as jnp
from jax import lax

HD = 64
HEADS = 32
BLOCK = 128
SPAN = 2048
SEQ = 16384
N_CTX = 8


def soft_pair(key):
    base = jax.random.fold_in(key, 7117)
    key_seed, query_seed = jax.random.split(base, 2)
    shape = (SEQ, HEADS * HD)
    keys = jnp.clip(jax.random.normal(key_seed, shape, jnp.float32), -6.0, 6.0)
    queries = jnp.clip(jax.random.normal(query_seed, shape, jnp.float32), -6.0, 6.0)
    return (queries, keys)


def draw_soft_query(key, part):
    return soft_pair(key)[0].astype(jnp.bfloat16)


def draw_soft_key(key, part):
    return soft_pair(key)[1].astype(jnp.bfloat16)


def draw_decays(key, part):
    seeds = jax.random.split(jax.random.fold_in(key, 311), 6)
    cutoff = 5
    fast = jax.random.randint(seeds[0], (HEADS,), 0, 10) < cutoff
    fast_rate = jnp.exp(jax.random.uniform(seeds[1], (HEADS,), jnp.float32, math.log(1.0 / 50.0), math.log(1.0 / 30.0)))
    slow_rate = 0.3 / SEQ * jax.random.uniform(seeds[2], (HEADS,), jnp.float32, 0.5, 1.0)
    baseline_decay_rate = jnp.where(fast, fast_rate, slow_rate)
    multiplier_value = jnp.exp(jax.random.uniform(seeds[3], (SEQ, HEADS), jnp.float32, math.log(0.5), math.log(2.0)))
    spots = jax.random.randint(seeds[4], (3, HEADS), 0, SEQ)
    spike_magnitude = -jnp.log(1.0 - jax.random.uniform(seeds[5], (3, HEADS), jnp.float32, 0.2, 0.4))
    matched_entries = jnp.arange(SEQ)[:, None, None] == spots[None]
    spike_positions = jnp.sum(jnp.where(matched_entries, spike_magnitude[None], 0.0), axis=1)
    return (baseline_decay_rate[None, :] * multiplier_value + spike_positions).astype(jnp.bfloat16)


def draw_block_mask(key, part):
    blocks = SPAN // BLOCK
    flags = jax.random.randint(jax.random.fold_in(key, 53), (SEQ // BLOCK, blocks), 0, 2)
    own = (jnp.arange(SEQ // BLOCK) % blocks)[:, None]
    column = jnp.arange(blocks)[None, :]
    return jnp.where(column == own, 1, jnp.where(column < own, flags, 0)).astype(jnp.int32)


def shard_levels(own_key, extent, shards, least, high):
    factor_of, own = 1.0, jax.random.fold_in(own_key, 6)
    for dim, parts in shards:
        steps = jnp.exp(jax.random.uniform(jax.random.fold_in(own, dim), (parts,), jnp.float32, least / len(shards), high / len(shards)))
        factor_of = factor_of * jnp.repeat(steps, extent[dim] // parts).reshape([-1 if axis == dim else 1 for axis in range(len(extent))])
    return factor_of


def scatter_about(rng, shape, scale, most, pieces=(), held_as=jnp.bfloat16):
    factor_of = shard_levels(rng, shape, pieces, -0.22, 0.18) if pieces else 1.0
    result = jax.random.normal(rng, shape, jnp.float32) * scale * factor_of
    return jnp.minimum(jnp.maximum(result, -most), most).astype(held_as)


def setup_inputs(seed: int = 0) -> dict:
    arg_keys = jax.random.split(jax.random.key(seed), 9)
    light_query = scatter_about(arg_keys[0], (SEQ, HEADS * HD), 1.0, 6.0, ((0, 32),))
    light_key = scatter_about(arg_keys[1], (SEQ, HEADS * HD), 1.0, 6.0, ((0, 32),))
    light_value = scatter_about(arg_keys[2], (SEQ, HEADS * HD), 1.0, 6.0, ((0, 32),))
    soft_query = draw_soft_query(jax.random.fold_in(arg_keys[8], 71), 0)
    soft_key = draw_soft_key(jax.random.fold_in(arg_keys[8], 71), 0)
    upstream = scatter_about(arg_keys[5], (SEQ, HEADS * HD), 1.0, 6.0, ((0, 32),))
    decays = draw_decays(jax.random.fold_in(arg_keys[8], 71), 0)
    block_mask = draw_block_mask(jax.random.fold_in(arg_keys[8], 71), 0)
    return dict(light_query=light_query, light_key=light_key, light_value=light_value, soft_query=soft_query, soft_key=soft_key, upstream=upstream, decays=decays, block_mask=block_mask)


HIGH = lax.Precision.HIGHEST

def combine_pairs(earlier, later):
    return (earlier[0] * later[0], later[0][:, None, None] * earlier[1] + later[1])

def span_tables(decay_rows):
    levels = jnp.cumsum(decay_rows.astype(jnp.float32).T, axis=1)
    count = levels.shape[1]
    places = jnp.arange(count)
    lower = places[None, :] <= places[:, None]
    spread = levels[:, None, :] - levels[:, :, None]
    weights = jnp.where(lower[None], jnp.exp(jnp.minimum(spread, 0.0)), 0.0)
    finals = levels[:, -1]
    entries = jnp.exp(-levels).T
    leaving = jnp.exp(levels - finals[:, None]).T
    return (weights, entries, leaving, jnp.exp(-finals))

def allowed_pairs(flags, count):
    places = jnp.arange(count)
    expanded = jnp.repeat(jnp.repeat(flags, BLOCK, axis=0), BLOCK, axis=1)
    return (expanded == 1) & (places[None, :] <= places[:, None])

def mixing(form, left, right):
    return jnp.einsum(form, left.astype(jnp.float32), right.astype(jnp.float32), precision=HIGH)

def exact(form, left, right):
    return jnp.einsum(form, left, right, precision=HIGH)

def summary_of(light_key, light_value, decay_blocks):
    weights, entries, leaving, running_totals = jax.vmap(span_tables)(decay_blocks)
    block_sums = exact('nshi,nshj->nhij', light_key.astype(jnp.float32) * leaving[..., None], light_value.astype(jnp.float32))
    return (running_totals, block_sums)

def middle_pass(light_query, soft_query, soft_key, upstream, decay_blocks, flags):
    weights, entries, leaving, running_totals = jax.vmap(span_tables)(decay_blocks)
    head_width = soft_query.shape[2]
    root = 1.0 / math.sqrt(head_width)
    allowed = allowed_pairs(flags, soft_query.shape[0])

    def one_head(items):
        query_per_head, key_h, cotan_h = items
        scores = mixing('td,sd->ts', query_per_head, key_h) * root
        scores = jnp.where(allowed, scores, -jnp.inf)
        highest = lax.optimization_barrier(jnp.max(scores, axis=-1, keepdims=True))
        powers = jnp.exp(scores - highest)
        probs = powers / lax.optimization_barrier(jnp.sum(powers, axis=-1, keepdims=True))
        probs_low = probs.astype(jnp.bfloat16)
        return mixing('ts,td->sd', probs_low, cotan_h).astype(jnp.bfloat16)
    lit_grad = lax.map(one_head, (jnp.transpose(soft_query, (1, 0, 2)), jnp.transpose(soft_key, (1, 0, 2)), jnp.transpose(upstream, (1, 0, 2))))
    lit_grad = jnp.transpose(lit_grad, (1, 0, 2)).reshape(light_query.shape)
    reach = exact('nthi,nthj->nhij', light_query.astype(jnp.float32) * entries[..., None], lit_grad.astype(jnp.float32))
    return (lit_grad, reach)

def last_pass(light_query, light_key, light_value, lit_grad, decay_blocks, state_in, reach_in):
    weights, entries, leaving, running_totals = jax.vmap(span_tables)(decay_blocks)
    head_width = light_query.shape[3]
    scale = 1.0 / (head_width * math.sqrt(head_width))
    mixed = (mixing('nthd,nshd->nhts', light_query, light_key) * weights).astype(jnp.bfloat16)
    back = (mixing('nthd,nshd->nhts', lit_grad, light_value) * weights).astype(jnp.bfloat16)
    grad_query = scale * (mixing('nhts,nshd->nthd', back, light_key) + entries[..., None] * exact('nthj,nhij->nthi', lit_grad.astype(jnp.float32), state_in))
    grad_key = scale * (mixing('nhts,nthd->nshd', back, light_query) + leaving[..., None] * exact('nshj,nhij->nshi', light_value.astype(jnp.float32), reach_in))
    grad_value = scale * (mixing('nhts,nthd->nshd', mixed, lit_grad) + leaving[..., None] * exact('nshi,nhij->nshj', light_key.astype(jnp.float32), reach_in))
    return (grad_query.astype(jnp.bfloat16), grad_key.astype(jnp.bfloat16), grad_value.astype(jnp.bfloat16))

def reference(light_query, light_key, light_value, soft_query, soft_key, upstream, decays, block_mask):
    blocks = SPAN // BLOCK
    shaped = (N_CTX, blocks, BLOCK, HEADS, HD)
    spanned = (N_CTX, SPAN, HEADS, HD)
    query_one = light_query.reshape(shaped)
    key_one = light_key.reshape(shaped)
    value_one = light_value.reshape(shaped)
    query_two = soft_query.reshape(spanned)
    key_two = soft_key.reshape(spanned)
    cotan = upstream.reshape(spanned)
    decay_all = decays.reshape(N_CTX, blocks, BLOCK, HEADS)
    flag_all = block_mask.reshape(N_CTX, blocks, blocks)

    def one_summary(items):
        return summary_of(items[0], items[1], items[2])
    running_totals, block_sums = lax.map(one_summary, (key_one, value_one, decay_all))
    running_totals = running_totals.reshape(N_CTX * blocks, HEADS)
    block_sums = block_sums.reshape(N_CTX * blocks, HEADS, HD, HD)
    identity = (jnp.ones((HEADS,), jnp.float32), jnp.zeros((HEADS, HD, HD), jnp.float32))

    def carry_step(carried, item):
        return (combine_pairs(carried, item), carried)
    _, prefix = lax.scan(carry_step, identity, (running_totals, block_sums))
    states = prefix[1].reshape(N_CTX, blocks, HEADS, HD, HD)

    def one_middle(items):
        return middle_pass(*items)
    lit_grads, reaches = lax.map(one_middle, (query_one, query_two, key_two, cotan, decay_all, flag_all))
    _, suffix = lax.scan(carry_step, identity, (running_totals, reaches.reshape(N_CTX * blocks, HEADS, HD, HD)), reverse=True)
    reach_ins = suffix[1].reshape(N_CTX, blocks, HEADS, HD, HD)

    def one_last(items):
        return last_pass(*items)
    grad_q_one, grad_k_one, grad_v_one = lax.map(one_last, (query_one, key_one, value_one, lit_grads, decay_all, states, reach_ins))
    flat = (SEQ, HEADS * HD)
    return (grad_q_one.reshape(flat), grad_k_one.reshape(flat), grad_v_one.reshape(flat))
```

```python
import functools
import math

import jax
import jax.numpy as jnp
from jax import lax
from jax.experimental import pallas as pl
from jax.experimental.pallas import tpu as pltpu
from jax.sharding import PartitionSpec as P

BLOCK = 128
BF = jnp.bfloat16
F32 = jnp.float32
NEG = -1e30
AXES = ("ctx", "head")


def mm(a, b, ca, cb):
    return lax.dot_general(a, b, (((ca,), (cb,)), ((), ())), preferred_element_type=F32)


def halves(x):
    top = x.astype(BF)
    return top, (x - top.astype(F32)).astype(BF)


def mm_left(x, b, ca, cb):
    top, rest = halves(x)
    return mm(top, b, ca, cb) + mm(rest, b, ca, cb)


def mm_right(a, x, ca, cb):
    top, rest = halves(x)
    return mm(a, top, ca, cb) + mm(a, rest, ca, cb)


def params(megabytes=48):
    return pltpu.CompilerParams(vmem_limit_bytes=megabytes * 2**20)


def lane_masks(width):
    lane = lax.broadcasted_iota(jnp.int32, (1, width), 1)
    left = (lane < width // 2).astype(F32).astype(BF)
    right = (lane >= width // 2).astype(F32).astype(BF)
    return left, right


def split_pair(x):
    left, right = lane_masks(x.shape[1])
    return jnp.concatenate([x * left, x * right], axis=0)


def pack_kernel(count, _, *refs):
    ins, outs = refs[: 3 * count], refs[3 * count :]
    for k in range(count):
        for n in range(3):
            outs[k][n] = ins[3 * k + n][...]


def pack(here, arrays, chunk, count, width):
    rows = arrays[0].shape[0]

    def spec(k):
        return pl.BlockSpec(
            (rows, width), lambda i, z: (0, chunk * count + lax.rem(z[0] + k, count))
        )

    return pl.pallas_call(
        functools.partial(pack_kernel, count),
        out_shape=[jax.ShapeDtypeStruct((3, rows, width), BF)] * count,
        grid_spec=pltpu.PrefetchScalarGridSpec(
            num_scalar_prefetch=1,
            grid=(1,),
            in_specs=[spec(k) for k in range(count) for _ in range(3)],
            out_specs=[pl.BlockSpec((3, rows, width), lambda i, z: (0, 0, 0))] * count,
        ),
        compiler_params=params(),
        cost_estimate=pl.CostEstimate(
            flops=0, transcendentals=0, bytes_accessed=12 * count * rows * width
        ),
        name="pack",
    )(here, *(array for _ in range(count) for array in arrays))


def soft_kernel(count, root, z_ref, flags, *refs):
    ins = refs[:count]
    outs = refs[count : 2 * count]
    queries, keys, cotans, scores, summed, listed = refs[2 * count :]
    rows, width = ins[0].shape[1:]
    z = z_ref[0]
    per = rows // BLOCK
    left, right = lane_masks(width)
    for k in range(count):
        owner = lax.rem(z - k + count, count)
        at = pl.ds(pl.multiple_of(owner * rows, rows), rows)
        queries[at, :] = ins[k][0] * jnp.asarray(root, BF)
        keys[at, :] = ins[k][1]
        cotans[at, :] = ins[k][2]
    summed[...] = jnp.zeros_like(summed)

    def rows_of(j):
        return pl.ds(pl.multiple_of(j * BLOCK, BLOCK), BLOCK)

    def query_block(i, _):
        query = split_pair(queries[rows_of(i), :])
        cotan = split_pair(cotans[rows_of(i), :])

        def collect(j, found):
            listed[found] = j
            return found + flags[i, j]

        found = lax.fori_loop(0, i, collect, 0)
        shape = (BLOCK, 2 * BLOCK)
        key_at = lax.broadcasted_iota(jnp.int32, shape, 0)
        query_at = lax.rem(lax.broadcasted_iota(jnp.int32, shape, 1), BLOCK)
        own = mm(keys[rows_of(i), :], query, 1, 1)
        own = jnp.where(key_at <= query_at, own, NEG)
        highest = jnp.max(own, axis=0, keepdims=True)

        def first(n, highest):
            block = mm(keys[rows_of(listed[n]), :], query, 1, 1)
            scores[rows_of(n), :] = block
            return jnp.maximum(highest, jnp.max(block, axis=0, keepdims=True))

        def first_two(n, highest):
            return first(2 * n + 1, first(2 * n, highest))

        highest = lax.fori_loop(0, found // 2, first_two, highest)
        highest = lax.fori_loop(2 * (found // 2), found, first, highest)
        own = jnp.exp(own - highest)
        total = jnp.sum(own, axis=0, keepdims=True)

        def second(n, total):
            block = jnp.exp(scores[rows_of(n), :] - highest)
            scores[rows_of(n), :] = block
            return total + jnp.sum(block, axis=0, keepdims=True)

        def second_two(n, total):
            return second(2 * n + 1, second(2 * n, total))

        total = lax.fori_loop(0, found // 2, second_two, total)
        total = lax.fori_loop(2 * (found // 2), found, second, total)
        share = 1.0 / total
        summed[rows_of(i), :] += mm((own * share).astype(BF), cotan, 1, 0)

        def third(n, _):
            block = (scores[rows_of(n), :] * share).astype(BF)
            summed[rows_of(listed[n]), :] += mm(block, cotan, 1, 0)
            return 0

        def third_two(n, _):
            blocks = [(scores[rows_of(2 * n + m), :] * share).astype(BF) for m in range(2)]
            parts = [mm(block, cotan, 1, 0) for block in blocks]
            for m in range(2):
                summed[rows_of(listed[2 * n + m]), :] += parts[m]
            return 0

        lax.fori_loop(0, found // 2, third_two, 0)
        lax.fori_loop(2 * (found // 2), found, third, 0)
        return 0

    lax.fori_loop(0, count * per, query_block, 0)
    for k in range(count):
        owner = lax.rem(z + k, count)
        at = pl.ds(pl.multiple_of(owner * rows, rows), rows)
        outs[k][...] = summed[at, :].astype(BF)


def soft(here, flags, pieces, root):
    count = len(pieces)
    rows, width = pieces[0].shape[1:]
    span = count * rows
    vmem = pl.BlockSpec(memory_space=pltpu.VMEM)
    smem = pl.BlockSpec(memory_space=pltpu.SMEM)
    return pl.pallas_call(
        functools.partial(soft_kernel, count, root),
        out_shape=[jax.ShapeDtypeStruct((rows, width), BF)] * count,
        in_specs=[smem, smem] + [vmem] * count,
        out_specs=[vmem] * count,
        scratch_shapes=[
            pltpu.VMEM((span, width), BF),
            pltpu.VMEM((span, width), BF),
            pltpu.VMEM((span, width), BF),
            pltpu.VMEM((span, 2 * BLOCK), F32),
            pltpu.VMEM((span, width), F32),
            pltpu.SMEM((span // BLOCK + 1,), jnp.int32),
        ],
        compiler_params=params(),
        cost_estimate=pl.CostEstimate(
            flops=4 * span * span * width, transcendentals=span * span, bytes_accessed=8 * span * width
        ),
        name="soft",
    )(here, flags, *pieces)


def triangle():
    row = lax.broadcasted_iota(jnp.int32, (BLOCK, BLOCK), 0)
    column = lax.broadcasted_iota(jnp.int32, (BLOCK, BLOCK), 1)
    return row >= column


def level_tables(decays, pair):
    heads = decays.shape[1]
    head = lax.broadcasted_iota(jnp.int32, (heads, 2 * BLOCK), 0)
    lane = lax.broadcasted_iota(jnp.int32, (heads, 2 * BLOCK), 1)
    spread = (head == 2 * pair + lane // BLOCK).astype(F32).astype(BF)
    wide = mm(decays, spread, 1, 0).astype(BF)
    levels = mm(triangle().astype(F32).astype(BF), wide, 1, 0)
    return levels[:, :BLOCK], levels[:, BLOCK:]


def by_lane(first, second):
    lane = lax.broadcasted_iota(jnp.int32, first.shape, 1)
    return jnp.where(lane < BLOCK // 2, first, second)


def on_diagonal(x):
    row = lax.broadcasted_iota(jnp.int32, x.shape, 0)
    lane = lax.broadcasted_iota(jnp.int32, x.shape, 1)
    half = BLOCK // 2
    return jnp.where((row < half) == (lane < half), x, 0.0)


def fold(x):
    return x[: BLOCK // 2] + x[BLOCK // 2 :]


def unfold(x):
    return on_diagonal(jnp.concatenate([x, x], axis=0))


def state_kernel(k_ref, v_ref, d_ref, sum_ref, total_ref):
    pair = pl.program_id(0)
    blocks = k_ref.shape[0] // BLOCK
    state = jnp.zeros((BLOCK, BLOCK), F32)
    whole = jnp.zeros((1, BLOCK), F32)
    for b in range(blocks):
        at = slice(b * BLOCK, (b + 1) * BLOCK)
        level = by_lane(*level_tables(d_ref[at, :], pair))
        last = level[BLOCK - 1 :]
        key = k_ref[at, :].astype(F32) * jnp.exp(level - last)
        state = jnp.exp(-last) * state + on_diagonal(mm_left(key, v_ref[at, :], 0, 0))
        whole = whole + last
    sum_ref[0] = fold(state)
    total_ref[0] = jnp.broadcast_to(jnp.exp(-whole), total_ref.shape[1:])


def device_state(light_key, light_value, decays, pairs):
    rows = light_key.shape[0]
    block = pl.BlockSpec((rows, BLOCK), lambda p: (0, p))
    return pl.pallas_call(
        state_kernel,
        out_shape=[
            jax.ShapeDtypeStruct((pairs, BLOCK // 2, BLOCK), F32),
            jax.ShapeDtypeStruct((pairs, 8, BLOCK), F32),
        ],
        grid=(pairs,),
        in_specs=[block, block, pl.BlockSpec(decays.shape, lambda p: (0, 0))],
        out_specs=[
            pl.BlockSpec((1, BLOCK // 2, BLOCK), lambda p: (p, 0, 0)),
            pl.BlockSpec((1, 8, BLOCK), lambda p: (p, 0, 0)),
        ],
        compiler_params=params(),
        cost_estimate=pl.CostEstimate(
            flops=8 * rows * pairs * BLOCK * BLOCK, transcendentals=rows * pairs * BLOCK, bytes_accessed=4 * rows * pairs * BLOCK
        ),
        name="state",
    )(light_key, light_value, decays)


def take_lit(count, z, lits, held):
    @pl.when(pl.program_id(0) == 0)
    def _():
        for k in range(count):
            held[lax.rem(z - k + count, count)] = lits[k][...]


def reach_kernel(count, chunk, z_ref, q_ref, d_ref, *refs):
    lits, (sum_ref, held) = refs[:count], refs[count:]
    take_lit(count, z_ref[0], lits, held)
    here = pl.program_id(0)
    blocks = q_ref.shape[0] // BLOCK
    state = jnp.zeros((BLOCK, BLOCK), F32)
    for b in reversed(range(blocks)):
        at = slice(b * BLOCK, (b + 1) * BLOCK)
        level = by_lane(*level_tables(d_ref[at, :], chunk * count + here))
        query = q_ref[at, :].astype(F32) * jnp.exp(-level)
        last = level[BLOCK - 1 :]
        state = jnp.exp(-last) * state + on_diagonal(mm_left(query, held[here, at, :], 0, 0))
    sum_ref[0] = fold(state)


def device_reach(here, light_query, decays, lits, chunk):
    count = len(lits)
    rows = light_query.shape[0]
    return pl.pallas_call(
        functools.partial(reach_kernel, count, chunk),
        out_shape=jax.ShapeDtypeStruct((count, BLOCK // 2, BLOCK), F32),
        grid_spec=pltpu.PrefetchScalarGridSpec(
            num_scalar_prefetch=1,
            grid=(count,),
            in_specs=[
                pl.BlockSpec((rows, BLOCK), lambda p, z: (0, chunk * count + p)),
                pl.BlockSpec(decays.shape, lambda p, z: (0, 0)),
            ]
            + [pl.BlockSpec((rows, BLOCK), lambda p, z: (0, 0))] * count,
            out_specs=pl.BlockSpec((1, BLOCK // 2, BLOCK), lambda p, z: (p, 0, 0)),
            scratch_shapes=[pltpu.VMEM((count, rows, BLOCK), BF)],
        ),
        compiler_params=params(),
        cost_estimate=pl.CostEstimate(
            flops=8 * rows * count * BLOCK * BLOCK, transcendentals=rows * count * BLOCK, bytes_accessed=4 * rows * count * BLOCK
        ),
        name="reach",
    )(here, light_query, decays, *lits)


def chain_kernel(reverse, x_ref, a_ref, o_ref):
    count = x_ref.shape[0]

    def step(n, carried):
        e = count - 1 - n if reverse else n
        o_ref[e] = carried
        return a_ref[e] * carried + x_ref[e]

    lax.fori_loop(0, count, step, jnp.zeros(x_ref.shape[1:], F32))


def chain(items, totals, reverse):
    vmem = pl.BlockSpec(memory_space=pltpu.VMEM)
    return pl.pallas_call(
        functools.partial(chain_kernel, reverse),
        out_shape=jax.ShapeDtypeStruct(items.shape, F32),
        in_specs=[vmem, vmem],
        out_specs=vmem,
        compiler_params=params(),
        cost_estimate=pl.CostEstimate(flops=2 * items.size, transcendentals=0, bytes_accessed=12 * items.size),
        name="chain",
    )(items, totals)


def final_kernel(count, chunk, scale, olds, z_ref, q_ref, k_ref, v_ref, d_ref, t_ref, s_ref, r_ref, *refs):
    lits = refs[:count]
    gq_ref, gk_ref, gv_ref, held = refs[count + olds :]
    take_lit(count, z_ref[0], lits, held)
    here = pl.program_id(0)
    blocks = q_ref.shape[0] // BLOCK
    lower = triangle()
    upper = jnp.logical_not(lower) | (
        lax.broadcasted_iota(jnp.int32, lower.shape, 0) == lax.broadcasted_iota(jnp.int32, lower.shape, 1)
    )
    upper = upper.astype(F32).astype(BF)
    state = unfold(s_ref[0])
    kept = []
    for b in range(blocks):
        at = slice(b * BLOCK, (b + 1) * BLOCK)
        query, key, value, lit = (q_ref[at, :], k_ref[at, :], v_ref[at, :], held[here, at, :])
        first, second = level_tables(d_ref[at, :], chunk * count + here)
        level = by_lane(first, second)
        last = level[BLOCK - 1 :]
        entries = jnp.exp(-level)
        leaving = jnp.exp(level - last)
        decay = jnp.exp(-last)
        lined = mm(t_ref[0, :, at].astype(BF), upper, 1, 0)
        weights = [
            jnp.where(lower, jnp.exp(jnp.minimum(row - column, 0.0)), 0.0)
            for row, column in ((lined[0:1], first), (lined[4:5], second))
        ]
        queries, keys, values, twice = (split_pair(query), split_pair(key), split_pair(value), split_pair(lit))
        mixed = mm(query, keys, 1, 1)
        back = mm(lit, values, 1, 1)
        mixed = [(mixed[:, n * BLOCK : (n + 1) * BLOCK] * weights[n]).astype(BF) for n in range(2)]
        back = [(back[:, n * BLOCK : (n + 1) * BLOCK] * weights[n]).astype(BF) for n in range(2)]
        grad_query = mm(jnp.concatenate(back, axis=1), keys, 1, 0) + entries * mm_right(lit, state, 1, 1)
        gq_ref[at, :] = (scale * grad_query).astype(BF)
        grad_key = mm(jnp.concatenate(back, axis=0), queries, 0, 0)
        grad_value = mm(jnp.concatenate(mixed, axis=0), twice, 0, 0)
        kept.append((grad_key, grad_value, entries, leaving, decay))
        if b < blocks - 1:
            state = decay * state + on_diagonal(mm_left(key.astype(F32) * leaving, value, 0, 0))
    state = unfold(r_ref[0])
    for b in reversed(range(blocks)):
        at = slice(b * BLOCK, (b + 1) * BLOCK)
        grad_key, grad_value, entries, leaving, decay = kept[b]
        grad_key = grad_key + leaving * mm_right(v_ref[at, :], state, 1, 1)
        grad_value = grad_value + leaving * mm_right(k_ref[at, :], state, 1, 0)
        gk_ref[at, :] = (scale * grad_key).astype(BF)
        gv_ref[at, :] = (scale * grad_value).astype(BF)
        if b > 0:
            query = q_ref[at, :].astype(F32) * entries
            state = decay * state + on_diagonal(mm_left(query, held[here, at, :], 0, 0))


def final(here, light_query, light_key, light_value, decays, lines, state_in, reach_in, lits, chunk, scale, olds):
    count = len(lits)
    rows, columns = light_query.shape
    block = pl.BlockSpec((rows, BLOCK), lambda p, z: (0, chunk * count + p))
    small = pl.BlockSpec((1, BLOCK // 2, BLOCK), lambda p, z: (p, 0, 0))
    base = 8 + count
    return pl.pallas_call(
        functools.partial(final_kernel, count, chunk, scale, len(olds)),
        out_shape=[jax.ShapeDtypeStruct((rows, columns), BF)] * 3,
        grid_spec=pltpu.PrefetchScalarGridSpec(
            num_scalar_prefetch=1,
            grid=(count,),
            in_specs=[
                block,
                block,
                block,
                pl.BlockSpec(decays.shape, lambda p, z: (0, 0)),
                pl.BlockSpec((1, 8, rows), lambda p, z: (chunk * count + p, 0, 0)),
                small,
                small,
            ]
            + [pl.BlockSpec((rows, BLOCK), lambda p, z: (0, 0))] * count
            + [pl.BlockSpec(memory_space=pl.ANY)] * len(olds),
            out_specs=[block] * 3,
            scratch_shapes=[pltpu.VMEM((count, rows, BLOCK), BF)],
        ),
        input_output_aliases={base + n: n for n in range(len(olds))},
        compiler_params=params(),
        cost_estimate=pl.CostEstimate(
            flops=40 * rows * count * BLOCK * BLOCK, transcendentals=4 * rows * count * BLOCK, bytes_accessed=14 * rows * count * BLOCK
        ),
        name="final",
    )(here, light_query, light_key, light_value, decays, lines, state_in, reach_in, *lits, *olds)


def turn(pieces, count):
    return [pieces[0]] + [
        lax.ppermute(pieces[k], "head", [(i, (i + k) % count) for i in range(count)])
        for k in range(1, count)
    ]


def body(light_query, light_key, light_value, soft_query, soft_key, upstream, decays, block_mask):
    count, spans = lax.axis_size("head"), lax.axis_size("ctx")
    devices = count * spans
    rows, columns = light_query.shape
    heads = decays.shape[1]
    head_width = columns // heads
    pairs = heads // 2
    chunks = pairs // count
    assert 2 * head_width == BLOCK and chunks * count == pairs
    part = head_width // spans
    assert part * spans == head_width
    scale = 1.0 / (head_width * math.sqrt(head_width))
    root = 1.0 / math.sqrt(head_width)
    here = lax.axis_index("head").astype(jnp.int32).reshape(1)
    block_mask = block_mask.astype(jnp.int32)

    packed = [
        turn(pack(here, (soft_query, soft_key, upstream), c, count, BLOCK), count) for c in range(chunks)
    ]
    sums, totals = device_state(light_key, light_value, decays, pairs)
    lines = jnp.repeat(decays.T.astype(F32).reshape(pairs, 2, rows), 4, axis=1)

    def exchange(x):
        return lax.all_to_all(x, AXES, split_axis=0, concat_axis=0, tiled=True)

    sends = jnp.swapaxes(sums.reshape(chunks, devices, part, BLOCK), 0, 1).reshape(devices, chunks * part, BLOCK)
    rates = jnp.repeat(jnp.swapaxes(totals[:, 0].reshape(chunks, count, BLOCK), 0, 1), spans, axis=0)
    got = exchange(jnp.concatenate([sends, rates], axis=1))
    rates = jnp.repeat(got[:, chunks * part :], part, axis=1)
    states = exchange(chain(got[:, : chunks * part], rates, False))
    states = jnp.swapaxes(states.reshape(devices, chunks, part, BLOCK), 0, 1)
    states = states.reshape(chunks, count, head_width, BLOCK)

    grads = ()
    for c in range(chunks):
        lits = turn(soft(here, block_mask, packed[c], root), count)
        reach = device_reach(here, light_query, decays, lits, c)
        got = exchange(reach.reshape(devices, part, BLOCK))
        reach_in = exchange(chain(got, rates[:, c * part : (c + 1) * part], True))
        grads = final(
            here, light_query, light_key, light_value, decays, lines, states[c],
            reach_in.reshape(count, head_width, BLOCK), lits, c, scale, tuple(grads),
        )
    return tuple(grads)


def solution(mesh):
    rows = P(AXES, None)
    return jax.shard_map(
        body,
        mesh=mesh,
        in_specs=(rows,) * 7 + (P("ctx", None),),
        out_specs=(rows,) * 3,
        check_vma=False,
    )
```

```python
import functools
import math

import jax
import jax.numpy as jnp
from jax import lax
from jax.experimental import pallas as pl
from jax.experimental.pallas import tpu as pltpu
from jax.sharding import PartitionSpec as P


BLOCK = 128
BF = jnp.bfloat16
F32 = jnp.float32
NEG = -1e30
AXES = ("ctx", "head")


def mm(a, b, ca, cb):
    return lax.dot_general(a, b, (((ca,), (cb,)), ((), ())), preferred_element_type=F32)


def params(megabytes=48):
    return pltpu.CompilerParams(vmem_limit_bytes=megabytes * 2**20)


def lane_masks(width):
    lane = lax.broadcasted_iota(jnp.int32, (1, width), 1)
    left = (lane < width // 2).astype(F32).astype(BF)
    right = (lane >= width // 2).astype(F32).astype(BF)
    return left, right


def split_pair(x):
    left, right = lane_masks(x.shape[1])
    return jnp.concatenate([x * left, x * right], axis=0)


def pack_kernel(count, _, *refs):
    ins, outs = refs[: 3 * count], refs[3 * count :]
    for k in range(count):
        for n in range(3):
            outs[k][n] = ins[3 * k + n][...]


def pack(here, arrays, chunk, count, width):
    rows = arrays[0].shape[0]

    def spec(k):
        return pl.BlockSpec(
            (rows, width), lambda i, z: (0, chunk * count + lax.rem(z[0] + k, count))
        )

    return pl.pallas_call(
        functools.partial(pack_kernel, count),
        out_shape=[jax.ShapeDtypeStruct((3, rows, width), BF)] * count,
        grid_spec=pltpu.PrefetchScalarGridSpec(
            num_scalar_prefetch=1,
            grid=(1,),
            in_specs=[spec(k) for k in range(count) for _ in range(3)],
            out_specs=[pl.BlockSpec((3, rows, width), lambda i, z: (0, 0, 0))] * count,
        ),
        compiler_params=params(),
        cost_estimate=pl.CostEstimate(
            flops=0, transcendentals=0, bytes_accessed=12 * count * rows * width
        ),
        name="pack",
    )(here, *(array for _ in range(count) for array in arrays))


def soft_kernel(count, root, z_ref, flags, *refs):
    ins = refs[:count]
    outs = refs[count : 2 * count]
    queries, keys, cotans, scores, tops, summed, listed = refs[2 * count :]
    rows, width = ins[0].shape[1:]
    z = z_ref[0]
    pairs = width // BLOCK
    groups = BLOCK // 8
    wide = 2 * BLOCK
    for k in range(count):
        owner = lax.rem(z - k + count, count)
        at = pl.ds(pl.multiple_of(owner * rows, rows), rows)
        queries[at, :] = ins[k][0] * jnp.asarray(root, BF)
        keys[at, :] = ins[k][1]
        cotans[at, :] = ins[k][2]
    summed[...] = jnp.zeros_like(summed)

    def rows_of(j):
        return pl.ds(pl.multiple_of(j * BLOCK, BLOCK), BLOCK)

    def lanes_of(p):
        return slice(p * BLOCK, (p + 1) * BLOCK)

    def query_block(i, _):
        query = [split_pair(queries[rows_of(i), lanes_of(p)]) for p in range(pairs)]
        cotan = [split_pair(cotans[rows_of(i), lanes_of(p)]) for p in range(pairs)]

        def collect(j, found):
            listed[found] = j
            return found + flags[i, j]

        listed[0] = i
        found = lax.fori_loop(0, i, collect, 1)
        key_at = lax.broadcasted_iota(jnp.int32, (BLOCK, wide), 0)
        query_at = lax.rem(lax.broadcasted_iota(jnp.int32, (BLOCK, wide), 1), BLOCK)

        def absorb(slots, p, blocks, top, total):
            newer = top
            for block in blocks:
                newer = jnp.maximum(newer, jnp.max(block, axis=0))
            total = total * jnp.exp(top - newer)
            for n, block in zip(slots, blocks):
                block = jnp.exp(block - newer[None])
                scores[p, n] = block
                tops[p, n] = newer
                total = total + jnp.sum(block, axis=0)
            return newer, total

        def raw(n, p):
            block = mm(keys[rows_of(listed[n]), lanes_of(p)], query[p], 1, 1)
            return block.reshape(groups, 8, wide)

        held = []
        for p in range(pairs):
            own = mm(keys[rows_of(i), lanes_of(p)], query[p], 1, 1)
            own = jnp.where(key_at <= query_at, own, NEG).reshape(groups, 8, wide)
            floor = jnp.full((8, wide), NEG, F32)
            held.append(absorb((0,), p, (own,), floor, jnp.zeros((8, wide), F32)))

        def first(unroll, start):
            def step(n, held):
                slots = [start + unroll * n + m for m in range(unroll)]
                blocks = [[raw(n, p) for n in slots] for p in range(pairs)]
                return tuple(absorb(slots, p, blocks[p], *held[p]) for p in range(pairs))

            return step

        twice = (found - 1) // 2
        held = lax.fori_loop(0, twice, first(2, 1), tuple(held))
        held = lax.fori_loop(2 * twice, found - 1, first(1, 1), held)
        highest, share = [], []
        for top, total in held:
            most = jnp.max(top, axis=0, keepdims=True)
            total = jnp.sum(total * jnp.exp(top - most), axis=0, keepdims=True)
            highest.append(most)
            share.append(1.0 / total)

        def second(unroll):
            def step(n, _):
                slots = [unroll * n + m for m in range(unroll)]
                parts = []
                for n in slots:
                    for p in range(pairs):
                        factor = jnp.exp(tops[p, n] - highest[p]) * share[p]
                        block = (scores[p, n] * factor[None]).reshape(BLOCK, wide).astype(BF)
                        parts.append((n, p, mm(block, cotan[p], 1, 0)))
                for n, p, part in parts:
                    summed[rows_of(listed[n]), lanes_of(p)] += part
                return 0

            return step

        twice = found // 2
        lax.fori_loop(0, twice, second(2), 0)
        lax.fori_loop(2 * twice, found, second(1), 0)
        return 0

    lax.fori_loop(0, count * (rows // BLOCK), query_block, 0)
    for k in range(count):
        owner = lax.rem(z + k, count)
        at = pl.ds(pl.multiple_of(owner * rows, rows), rows)
        outs[k][...] = summed[at, :].astype(BF)


def soft(here, flags, pieces, root):
    count = len(pieces)
    rows, width = pieces[0].shape[1:]
    span = count * rows
    vmem = pl.BlockSpec(memory_space=pltpu.VMEM)
    smem = pl.BlockSpec(memory_space=pltpu.SMEM)
    return pl.pallas_call(
        functools.partial(soft_kernel, count, root),
        out_shape=[jax.ShapeDtypeStruct((rows, width), BF)] * count,
        in_specs=[smem, smem] + [vmem] * count,
        out_specs=[vmem] * count,
        scratch_shapes=[
            pltpu.VMEM((span, width), BF),
            pltpu.VMEM((span, width), BF),
            pltpu.VMEM((span, width), BF),
            pltpu.VMEM((width // BLOCK, span // BLOCK, BLOCK // 8, 8, 2 * BLOCK), F32),
            pltpu.VMEM((width // BLOCK, span // BLOCK, 8, 2 * BLOCK), F32),
            pltpu.VMEM((span, width), F32),
            pltpu.SMEM((span // BLOCK + 1,), jnp.int32),
        ],
        compiler_params=params(),
        cost_estimate=pl.CostEstimate(
            flops=4 * span * span * width, transcendentals=span * span, bytes_accessed=8 * span * width
        ),
        name="soft",
    )(here, flags, *pieces)


def triangle():
    row = lax.broadcasted_iota(jnp.int32, (BLOCK, BLOCK), 0)
    column = lax.broadcasted_iota(jnp.int32, (BLOCK, BLOCK), 1)
    return row >= column


def spread_decays(decays, first, width, each):
    heads = decays.shape[1]
    head = lax.broadcasted_iota(jnp.int32, (heads, width), 0)
    lane = lax.broadcasted_iota(jnp.int32, (heads, width), 1)
    spread = (head == first + lane // each).astype(F32).astype(BF)
    return mm(decays, spread, 1, 0).astype(BF)


def device_levels(decays, first, width):
    wide = spread_decays(decays, first, width, BLOCK // 2)
    lower = triangle().astype(F32).astype(BF)
    before = jnp.zeros((1, width), F32)
    levels = []
    for b in range(decays.shape[0] // BLOCK):
        level = mm(lower, wide[b * BLOCK : (b + 1) * BLOCK], 1, 0)
        levels.append(level + before)
        before = before + level[BLOCK - 1 :]
    return jnp.concatenate(levels, axis=0), before


def by_lane(first, second):
    lane = lax.broadcasted_iota(jnp.int32, first.shape, 1)
    return jnp.where(lane < BLOCK // 2, first, second)


def on_diagonal(x):
    row = lax.broadcasted_iota(jnp.int32, x.shape, 0)
    lane = lax.broadcasted_iota(jnp.int32, x.shape, 1)
    half = BLOCK // 2
    return jnp.where((row < half) == (lane < half), x, 0.0)


def fold(x):
    return x[: BLOCK // 2] + x[BLOCK // 2 :]


def state_kernel(q_ref, k_ref, v_ref, d_ref, sum_ref, total_ref, scaled_ref):
    level, last = device_levels(d_ref[...], 2 * pl.program_id(0), BLOCK)
    key = (k_ref[...].astype(F32) * jnp.exp(level - last)).astype(BF)
    sum_ref[0] = fold(on_diagonal(mm(key, v_ref[...], 0, 0))).astype(BF)
    total_ref[0] = jnp.broadcast_to(last, total_ref.shape[1:])
    scaled_ref[...] = (q_ref[...].astype(F32) * jnp.exp(-level)).astype(BF)


def device_state(light_query, light_key, light_value, decays, pairs):
    rows = light_key.shape[0]
    block = pl.BlockSpec((rows, BLOCK), lambda p: (0, p))
    return pl.pallas_call(
        state_kernel,
        out_shape=[
            jax.ShapeDtypeStruct((pairs, BLOCK // 2, BLOCK), BF),
            jax.ShapeDtypeStruct((pairs, 8, BLOCK), F32),
            jax.ShapeDtypeStruct(light_query.shape, BF),
        ],
        grid=(pairs,),
        in_specs=[block, block, block, pl.BlockSpec(decays.shape, lambda p: (0, 0))],
        out_specs=[
            pl.BlockSpec((1, BLOCK // 2, BLOCK), lambda p: (p, 0, 0)),
            pl.BlockSpec((1, 8, BLOCK), lambda p: (p, 0, 0)),
            block,
        ],
        compiler_params=params(),
        cost_estimate=pl.CostEstimate(
            flops=8 * rows * pairs * BLOCK * BLOCK, transcendentals=rows * pairs * BLOCK, bytes_accessed=8 * rows * pairs * BLOCK
        ),
        name="state",
    )(light_query, light_key, light_value, decays)


def take_lit(count, z, lits, held):
    @pl.when(pl.program_id(0) == 0)
    def _():
        per = lits[0].shape[1] // BLOCK
        for k in range(count):
            owner = lax.rem(z - k + count, count)
            for p in range(per):
                held[owner * per + p] = lits[k][:, p * BLOCK : (p + 1) * BLOCK]


def reach_kernel(count, z_ref, q_ref, *refs):
    lits, sum_ref = refs[:count], refs[count]
    _, width = lits[0].shape
    per = width // BLOCK
    for k in range(count):
        owner = lax.rem(z_ref[0] - k + count, count)
        for p in range(per):
            at = pl.ds(pl.multiple_of((owner * per + p) * BLOCK, BLOCK), BLOCK)
            product = mm(q_ref[:, at], lits[k][:, p * BLOCK : (p + 1) * BLOCK], 0, 0)
            sum_ref[owner * per + p] = fold(on_diagonal(product)).astype(BF)


def device_reach(here, scaled, lits, chunk):
    count = len(lits)
    rows, width = lits[0].shape
    pairs = count * width // BLOCK
    return pl.pallas_call(
        functools.partial(reach_kernel, count),
        out_shape=jax.ShapeDtypeStruct((pairs, BLOCK // 2, BLOCK), BF),
        grid_spec=pltpu.PrefetchScalarGridSpec(
            num_scalar_prefetch=1,
            grid=(1,),
            in_specs=[pl.BlockSpec((rows, count * width), lambda p, z: (0, chunk))]
            + [pl.BlockSpec((rows, width), lambda p, z: (0, 0))] * count,
            out_specs=pl.BlockSpec((pairs, BLOCK // 2, BLOCK), lambda p, z: (0, 0, 0)),
        ),
        compiler_params=params(),
        cost_estimate=pl.CostEstimate(
            flops=2 * rows * pairs * BLOCK * BLOCK, transcendentals=0, bytes_accessed=4 * rows * pairs * BLOCK
        ),
        name="reach",
    )(here, scaled, *lits)


def chain_kernel(x_ref, a_ref, o_ref):
    count, half = x_ref.shape[0], x_ref.shape[1] // 2
    zero = jnp.zeros((half, x_ref.shape[2]), F32)

    def step(n, carried):
        early, late = carried
        m = count - 1 - n
        o_ref[n, :half, :] = early.astype(BF)
        o_ref[m, half:, :] = late.astype(BF)
        early = a_ref[n] * early + x_ref[n, :half, :].astype(F32)
        late = a_ref[m] * late + x_ref[m, half:, :].astype(F32)
        return early, late

    lax.fori_loop(0, count, step, (zero, zero))


def chain(items, totals):
    vmem = pl.BlockSpec(memory_space=pltpu.VMEM)
    return pl.pallas_call(
        chain_kernel,
        out_shape=jax.ShapeDtypeStruct(items.shape, BF),
        in_specs=[vmem, vmem],
        out_specs=vmem,
        compiler_params=params(),
        cost_estimate=pl.CostEstimate(flops=2 * items.size, transcendentals=0, bytes_accessed=8 * items.size),
        name="chain",
    )(items, totals)


def local_kernel(count, first_pair, skip, olds, z_ref, q_ref, k_ref, v_ref, d_ref, t_ref, *refs):
    lits = refs[:count]
    gq_ref, gk_ref, gv_ref, lit_ref, held = refs[count + olds :]
    take_lit(count, z_ref[0], lits, held)
    here = pl.program_id(0)
    blocks = q_ref.shape[0] // BLOCK
    shape = (BLOCK, BLOCK)
    row_at = lax.broadcasted_iota(jnp.int32, shape, 0)
    lane_at = lax.broadcasted_iota(jnp.int32, shape, 1)
    lower, upper = row_at >= lane_at, row_at <= lane_at
    ones_lower, ones_upper = (side.astype(F32).astype(BF) for side in (lower, upper))
    slot = skip + here
    spread = spread_decays(d_ref[...], 2 * (first_pair + slot), 2 * BLOCK, BLOCK)
    lines = t_ref[0].astype(BF)
    lit_ref[...] = held[slot]
    state = None
    kept = []
    for b in range(blocks):
        at = slice(b * BLOCK, (b + 1) * BLOCK)
        query, key, value, lit = (q_ref[at, :], k_ref[at, :], v_ref[at, :], held[slot, at, :])
        levels = mm(ones_lower, spread[at], 1, 0)
        lined = mm(lines[:, at], ones_upper, 1, 0)
        columns = (levels[:, :BLOCK], levels[:, BLOCK:])
        level = by_lane(*columns)
        last = level[BLOCK - 1 :]
        entries = jnp.exp(-level)
        leaving = jnp.exp(level - last)
        decay = jnp.exp(-last)
        spans = [lined[4 * n : 4 * n + 1] - columns[n] for n in range(2)]
        weights = jnp.concatenate(
            [jnp.where(lower, jnp.exp(jnp.minimum(span, 0.0)), 0.0) for span in spans], axis=1
        )
        turned = jnp.concatenate(
            [jnp.where(upper, jnp.exp(jnp.minimum(-span, 0.0)), 0.0) for span in spans], axis=1
        )
        queries, keys, values, twice = (split_pair(query), split_pair(key), split_pair(value), split_pair(lit))
        back = (mm(lit, values, 1, 1) * weights).astype(BF)
        back_turned = (mm(value, twice, 1, 1) * turned).astype(BF)
        mixed_turned = (mm(key, queries, 1, 1) * turned).astype(BF)
        grad_query = mm(back, keys, 1, 0)
        if state is not None:
            grad_query = grad_query + entries * mm(lit, state.astype(BF), 1, 1)
        gq_ref[at, :] = grad_query
        grad_key = mm(back_turned, queries, 1, 0)
        grad_value = mm(mixed_turned, twice, 1, 0)
        kept.append((grad_key, grad_value, entries, leaving, decay))
        if b < blocks - 1:
            left = (key.astype(F32) * leaving).astype(BF)
            left = on_diagonal(mm(left, value, 0, 0))
            state = left if state is None else decay * state + left
    state = None
    for b in reversed(range(blocks)):
        at = slice(b * BLOCK, (b + 1) * BLOCK)
        grad_key, grad_value, entries, leaving, decay = kept[b]
        if state is not None:
            low = state.astype(BF)
            grad_key = grad_key + leaving * mm(v_ref[at, :], low, 1, 1)
            grad_value = grad_value + leaving * mm(k_ref[at, :], low, 1, 0)
        gk_ref[at, :] = grad_key
        gv_ref[at, :] = grad_value
        if b > 0:
            query = (q_ref[at, :].astype(F32) * entries).astype(BF)
            query = on_diagonal(mm(query, held[slot, at, :], 0, 0))
            state = query if state is None else decay * state + query


def local(here, light_query, light_key, light_value, decays, lines, lits, first, skip, many, olds):
    count = len(lits)
    rows, columns = light_query.shape
    width = lits[0].shape[1]
    pairs = count * width // BLOCK
    block = pl.BlockSpec((rows, BLOCK), lambda p, z: (0, first + skip + p))
    base = 6 + count
    return pl.pallas_call(
        functools.partial(local_kernel, count, first, skip, len(olds)),
        out_shape=[jax.ShapeDtypeStruct((rows, columns), F32)] * 3 + [jax.ShapeDtypeStruct((rows, columns), BF)],
        grid_spec=pltpu.PrefetchScalarGridSpec(
            num_scalar_prefetch=1,
            grid=(many,),
            in_specs=[
                block,
                block,
                block,
                pl.BlockSpec(decays.shape, lambda p, z: (0, 0)),
                pl.BlockSpec((1, 8, rows), lambda p, z: (first + skip + p, 0, 0)),
            ]
            + [pl.BlockSpec((rows, width), lambda p, z: (0, 0))] * count
            + [pl.BlockSpec(memory_space=pl.ANY)] * len(olds),
            out_specs=[block] * 4,
            scratch_shapes=[pltpu.VMEM((pairs, rows, BLOCK), BF)],
        ),
        input_output_aliases={base + n: n for n in range(len(olds))},
        compiler_params=params(),
        cost_estimate=pl.CostEstimate(
            flops=40 * rows * many * BLOCK * BLOCK, transcendentals=4 * rows * many * BLOCK, bytes_accessed=22 * rows * many * BLOCK
        ),
        name="local",
    )(here, light_query, light_key, light_value, decays, lines, *lits, *olds)


def wide_state(x):
    pairs = x.shape[0]
    width = pairs * BLOCK
    x = jnp.concatenate([x[p] for p in range(pairs)], axis=1)
    x = jnp.concatenate([x] * (2 * pairs), axis=0)
    half = BLOCK // 2
    row = lax.broadcasted_iota(jnp.int32, (width, width), 0) // half
    lane = lax.broadcasted_iota(jnp.int32, (width, width), 1) // half
    return x * (row == lane).astype(F32).astype(BF)


def final_kernel(scale, pq_ref, pk_ref, pv_ref, lit_ref, k_ref, v_ref, d_ref, s_ref, r_ref, gq_ref, gk_ref, gv_ref):
    pairs = s_ref.shape[0]
    width = pairs * BLOCK
    level, last = device_levels(d_ref[...], 2 * pairs * pl.program_id(0), width)
    entries = scale * jnp.exp(-level)
    leaving = scale * jnp.exp(level - last)
    state, reach = wide_state(s_ref[...]), wide_state(r_ref[...])
    gq_ref[...] = (scale * pq_ref[...] + entries * mm(lit_ref[...], state, 1, 1)).astype(BF)
    gk_ref[...] = (scale * pk_ref[...] + leaving * mm(v_ref[...], reach, 1, 1)).astype(BF)
    gv_ref[...] = (scale * pv_ref[...] + leaving * mm(k_ref[...], reach, 1, 0)).astype(BF)


def final(parts, light_key, light_value, decays, state_in, reach_in, scale):
    rows, columns = light_key.shape
    pairs = columns // BLOCK
    step = 2 if pairs % 2 == 0 else 1
    block = pl.BlockSpec((rows, step * BLOCK), lambda p: (0, p))
    small = pl.BlockSpec((step, BLOCK // 2, BLOCK), lambda p: (p, 0, 0))
    return pl.pallas_call(
        functools.partial(final_kernel, scale),
        out_shape=[jax.ShapeDtypeStruct((rows, columns), BF)] * 3,
        grid=(pairs // step,),
        in_specs=[block] * 6 + [pl.BlockSpec(decays.shape, lambda p: (0, 0)), small, small],
        out_specs=[block] * 3,
        compiler_params=params(),
        cost_estimate=pl.CostEstimate(
            flops=6 * rows * columns * BLOCK, transcendentals=2 * rows * columns, bytes_accessed=24 * rows * columns
        ),
        name="final",
    )(*parts, light_key, light_value, decays, state_in, reach_in)


def turn(pieces, count):
    return [pieces[0]] + [
        lax.ppermute(pieces[k], "head", [(i, (i + k) % count) for i in range(count)])
        for k in range(1, count)
    ]


def program(light_query, light_key, light_value, soft_query, soft_key, upstream, decays, block_mask):
    count, spans = lax.axis_size("head"), lax.axis_size("ctx")
    devices = count * spans
    rows, columns = light_query.shape
    heads = decays.shape[1]
    head_width = columns // heads
    pairs = heads // 2
    share = pairs // count
    chunks = 2 if share % 2 == 0 else 1
    per = share // chunks
    assert 2 * head_width == BLOCK and share * count == pairs
    part = count * per * head_width // devices
    again = head_width // part
    assert part * again == head_width
    scale = 1.0 / (head_width * math.sqrt(head_width))
    root = 1.0 / math.sqrt(head_width)
    here = lax.axis_index("head").astype(jnp.int32).reshape(1)

    packed = []
    for c in range(chunks):
        pieces = pack(here, (soft_query, soft_key, upstream), c, count, per * BLOCK)
        packed.append(turn(pieces, count))
    sums, totals, scaled = device_state(light_query, light_key, light_value, decays, pairs)
    lines = jnp.repeat(decays.T.astype(F32).reshape(pairs, 2, rows), 4, axis=1)

    parts, reaches = (), []
    for c in range(chunks):
        lits = soft(here, block_mask, packed[c], root)
        lits = turn(lits, count)
        reaches.append(device_reach(here, scaled, lits, c))
        first, many = c * count * per, count * per
        cuts = (0, many // 2, many) if c == chunks - 1 else (0, many)
        for n in range(len(cuts) - 1):
            parts = local(
                here, light_query, light_key, light_value, decays, lines, lits, first,
                cuts[n], cuts[n + 1] - cuts[n], tuple(parts),
            )

    def exchange(x):
        return lax.all_to_all(x, AXES, split_axis=0, concat_axis=0, tiled=True)

    def spread(x):
        x = x.reshape(chunks, devices, part, BLOCK)
        return jnp.swapaxes(x, 0, 1).reshape(devices, chunks * part, BLOCK)

    def gather(x):
        x = x.reshape(devices, chunks, part, BLOCK)
        return jnp.swapaxes(x, 0, 1).reshape(pairs, head_width, BLOCK)

    rates = jnp.swapaxes(totals[:, 0].reshape(chunks, count * per, BLOCK), 0, 1)
    rates = jnp.repeat(rates, again, axis=0)
    thirds = []
    for _ in range(3):
        thirds.append(lax.reduce_precision(rates, 8, 7))
        rates = rates - thirds[-1]
    thirds = jnp.stack(thirds, axis=1).reshape(devices, 3 * chunks, BLOCK).astype(BF)
    half = chunks * part
    fill = jnp.zeros((devices, -(2 * half + 3 * chunks) % 8, BLOCK), BF)
    sends = [spread(sums), spread(jnp.concatenate(reaches, axis=0)), thirds, fill]
    got = exchange(jnp.concatenate(sends, axis=1))
    thirds = got[:, 2 * half : 2 * half + 3 * chunks].astype(F32).reshape(devices, 3, chunks, BLOCK)
    rates = jnp.exp(-(thirds[:, 0] + thirds[:, 1] + thirds[:, 2]))
    rates = jnp.repeat(rates, part, axis=1)
    given = chain(got[:, : 2 * half], rates)
    given = exchange(given)
    return tuple(
        final(parts, light_key, light_value, decays, gather(given[:, :half]), gather(given[:, half:]), scale)
    )


def solution(mesh):
    rows = P(AXES, None)
    return jax.shard_map(
        program,
        mesh=mesh,
        in_specs=(rows,) * 7 + (P("ctx", None),),
        out_specs=(rows,) * 3,
        check_vma=False,
    )
```

```python
import functools
import math

import jax
import jax.numpy as jnp
from jax import lax
from jax.experimental import pallas as pl
from jax.experimental.pallas import tpu as pltpu
from jax.sharding import PartitionSpec as P


BLOCK = 128
BF = jnp.bfloat16
F32 = jnp.float32
NEG = -1e30
AXES = ("ctx", "head")


def mm(a, b, ca, cb):
    return lax.dot_general(a, b, (((ca,), (cb,)), ((), ())), preferred_element_type=F32)


def params(megabytes=48):
    return pltpu.CompilerParams(vmem_limit_bytes=megabytes * 2**20)


def lane_masks(width):
    lane = lax.broadcasted_iota(jnp.int32, (1, width), 1)
    left = (lane < width // 2).astype(F32).astype(BF)
    right = (lane >= width // 2).astype(F32).astype(BF)
    return left, right


def split_pair(x):
    left, right = lane_masks(x.shape[1])
    return jnp.concatenate([x * left, x * right], axis=0)


def pack_kernel(count, _, *refs):
    ins, outs = refs[: 3 * count], refs[3 * count :]
    for k in range(count):
        for n in range(3):
            outs[k][n] = ins[3 * k + n][...]


def pack(here, arrays, chunk, count, width):
    rows = arrays[0].shape[0]

    def spec(k):
        return pl.BlockSpec(
            (rows, width), lambda i, z: (0, chunk * count + lax.rem(z[0] + k, count))
        )

    return pl.pallas_call(
        functools.partial(pack_kernel, count),
        out_shape=[jax.ShapeDtypeStruct((3, rows, width), BF)] * count,
        grid_spec=pltpu.PrefetchScalarGridSpec(
            num_scalar_prefetch=1,
            grid=(1,),
            in_specs=[spec(k) for k in range(count) for _ in range(3)],
            out_specs=[pl.BlockSpec((3, rows, width), lambda i, z: (0, 0, 0))] * count,
        ),
        compiler_params=params(),
        cost_estimate=pl.CostEstimate(
            flops=0, transcendentals=0, bytes_accessed=12 * count * rows * width
        ),
        name="pack",
    )(here, *(array for _ in range(count) for array in arrays))


def soft_kernel(count, root, z_ref, flags, *refs):
    ins = refs[:count]
    outs = refs[count : 2 * count]
    queries, keys, cotans, scores, tops, summed, listed = refs[2 * count :]
    rows, width = ins[0].shape[1:]
    z = z_ref[0]
    pairs = width // BLOCK
    groups = BLOCK // 8
    wide = 2 * BLOCK
    for k in range(count):
        owner = lax.rem(z - k + count, count)
        at = pl.ds(pl.multiple_of(owner * rows, rows), rows)
        queries[at, :] = ins[k][0] * jnp.asarray(root, BF)
        keys[at, :] = ins[k][1]
        cotans[at, :] = ins[k][2]
    summed[...] = jnp.zeros_like(summed)

    def rows_of(j):
        return pl.ds(pl.multiple_of(j * BLOCK, BLOCK), BLOCK)

    def lanes_of(p):
        return slice(p * BLOCK, (p + 1) * BLOCK)

    def query_block(i, _):
        query = [split_pair(queries[rows_of(i), lanes_of(p)]) for p in range(pairs)]
        cotan = [split_pair(cotans[rows_of(i), lanes_of(p)]) for p in range(pairs)]

        def collect(j, found):
            listed[found] = j
            return found + flags[i, j]

        listed[0] = i
        found = lax.fori_loop(0, i, collect, 1)
        key_at = lax.broadcasted_iota(jnp.int32, (BLOCK, wide), 0)
        query_at = lax.rem(lax.broadcasted_iota(jnp.int32, (BLOCK, wide), 1), BLOCK)

        def absorb(slots, p, blocks, top, total):
            newer = top
            for block in blocks:
                newer = jnp.maximum(newer, jnp.max(block, axis=0))
            total = total * jnp.exp(top - newer)
            for n, block in zip(slots, blocks):
                block = jnp.exp(block - newer[None])
                scores[p, n] = block
                tops[p, n] = newer
                total = total + jnp.sum(block, axis=0)
            return newer, total

        def raw(n, p):
            block = mm(keys[rows_of(listed[n]), lanes_of(p)], query[p], 1, 1)
            return block.reshape(groups, 8, wide)

        held = []
        for p in range(pairs):
            own = mm(keys[rows_of(i), lanes_of(p)], query[p], 1, 1)
            own = jnp.where(key_at <= query_at, own, NEG).reshape(groups, 8, wide)
            floor = jnp.full((8, wide), NEG, F32)
            held.append(absorb((0,), p, (own,), floor, jnp.zeros((8, wide), F32)))

        def first(unroll, start):
            def step(n, held):
                slots = [start + unroll * n + m for m in range(unroll)]
                blocks = [[raw(n, p) for n in slots] for p in range(pairs)]
                return tuple(absorb(slots, p, blocks[p], *held[p]) for p in range(pairs))

            return step

        twice = (found - 1) // 2
        held = lax.fori_loop(0, twice, first(2, 1), tuple(held))
        held = lax.fori_loop(2 * twice, found - 1, first(1, 1), held)
        highest, share = [], []
        for top, total in held:
            most = jnp.max(top, axis=0, keepdims=True)
            total = jnp.sum(total * jnp.exp(top - most), axis=0, keepdims=True)
            highest.append(most)
            share.append(1.0 / total)

        def second(unroll):
            def step(n, _):
                slots = [unroll * n + m for m in range(unroll)]
                parts = []
                for n in slots:
                    for p in range(pairs):
                        factor = jnp.exp(tops[p, n] - highest[p]) * share[p]
                        block = (scores[p, n] * factor[None]).reshape(BLOCK, wide).astype(BF)
                        parts.append((n, p, mm(block, cotan[p], 1, 0)))
                for n, p, part in parts:
                    summed[rows_of(listed[n]), lanes_of(p)] += part
                return 0

            return step

        twice = found // 2
        lax.fori_loop(0, twice, second(2), 0)
        lax.fori_loop(2 * twice, found, second(1), 0)
        return 0

    lax.fori_loop(0, count * (rows // BLOCK), query_block, 0)
    for k in range(count):
        owner = lax.rem(z + k, count)
        at = pl.ds(pl.multiple_of(owner * rows, rows), rows)
        outs[k][...] = summed[at, :].astype(BF)


def soft(here, flags, pieces, root):
    count = len(pieces)
    rows, width = pieces[0].shape[1:]
    span = count * rows
    vmem = pl.BlockSpec(memory_space=pltpu.VMEM)
    smem = pl.BlockSpec(memory_space=pltpu.SMEM)
    return pl.pallas_call(
        functools.partial(soft_kernel, count, root),
        out_shape=[jax.ShapeDtypeStruct((rows, width), BF)] * count,
        in_specs=[smem, smem] + [vmem] * count,
        out_specs=[vmem] * count,
        scratch_shapes=[
            pltpu.VMEM((span, width), BF),
            pltpu.VMEM((span, width), BF),
            pltpu.VMEM((span, width), BF),
            pltpu.VMEM((width // BLOCK, span // BLOCK, BLOCK // 8, 8, 2 * BLOCK), F32),
            pltpu.VMEM((width // BLOCK, span // BLOCK, 8, 2 * BLOCK), F32),
            pltpu.VMEM((span, width), F32),
            pltpu.SMEM((span // BLOCK + 1,), jnp.int32),
        ],
        compiler_params=params(),
        cost_estimate=pl.CostEstimate(
            flops=4 * span * span * width, transcendentals=span * span, bytes_accessed=8 * span * width
        ),
        name="soft",
    )(here, flags, *pieces)


OWNED = ((0, 1), (), (2, 3, 4), (5, 6, 7))
SHARE = 8
UNROLLS = {2: (4, 2, 1), 3: (4, 2, 1), 8: (2, 1)}


def pack_quad_kernel(z_ref, *refs):
    ins, outs = refs[:21], refs[21:]
    two, three, key_c, key_d, key_all, key_two = outs
    for n in range(3):
        two[n] = ins[n][...]
        for p in range(3):
            three[n, :, p * BLOCK : (p + 1) * BLOCK] = ins[3 + 3 * n + p][...]
        key_c[:, n * BLOCK : (n + 1) * BLOCK] = ins[12 + n][...]
        key_d[:, n * BLOCK : (n + 1) * BLOCK] = ins[15 + n][...]
    key_all[...] = ins[18][...]
    key_two[...] = ins[19][...]


def pack_quad(here, arrays, chunk):
    rows = arrays[0].shape[0]
    key = arrays[1]

    def spec(pair_of):
        return pl.BlockSpec((rows, BLOCK), lambda i, z: (0, SHARE * chunk + pair_of(z[0])))

    def far(p):
        return spec(lambda z: 5 - 3 * lax.div(z, 3) + p)

    front = pl.BlockSpec((rows, 2 * BLOCK), lambda i, z: (0, SHARE // 2 * chunk))
    operands = list(arrays) + [array for array in arrays for _ in range(3)] + [key] * 9
    specs = [front] * 3
    specs += [far(p) for p in range(3)] * 3
    specs += [spec(lambda z, p=p: 2 + 3 * jnp.minimum(z, 1) + p) for p in range(3)]
    specs += [spec(lambda z, p=p: 5 - 3 * jnp.minimum(z, 1) + p) for p in range(3)]
    specs += [pl.BlockSpec((rows, SHARE * BLOCK), lambda i, z: (0, chunk))]
    specs += [front] * 2
    shapes = [
        (3, rows, 2 * BLOCK), (3, rows, 3 * BLOCK), (rows, 3 * BLOCK), (rows, 3 * BLOCK),
        (rows, SHARE * BLOCK), (rows, 2 * BLOCK),
    ]
    return pl.pallas_call(
        pack_quad_kernel,
        out_shape=[jax.ShapeDtypeStruct(shape, BF) for shape in shapes],
        grid_spec=pltpu.PrefetchScalarGridSpec(
            num_scalar_prefetch=1,
            grid=(1,),
            in_specs=specs,
            out_specs=[pl.BlockSpec(shape, lambda i, z, n=len(shape): (0,) * n) for shape in shapes],
        ),
        compiler_params=params(60),
        cost_estimate=pl.CostEstimate(flops=0, transcendentals=0, bytes_accessed=120 * rows * BLOCK),
        name="pack",
    )(here, *operands)


def send(x, *routes):
    return lax.ppermute(x, "head", routes)


def turn_in(pieces):
    two, three, key_c, key_d, key_all, key_two = pieces
    return (
        send(three, (3, 2), (2, 3)),
        send(key_all, (0, 1)),
        send(key_c, (0, 2), (1, 3)),
        send(key_d, (0, 3), (1, 2)),
        send(two, (2, 0)),
        send(two, (3, 0)),
        send(key_two, (1, 0)),
    )


def turn_out(pieces):
    wide, three_d, three_e, three_f, two_a, two_b, two_c = pieces
    return (
        send(wide, (1, 0)),
        send(three_d, (2, 0), (3, 1)),
        send(three_e, (2, 1), (3, 0)),
        send(three_f, (2, 3), (3, 2)),
        send(two_a, (0, 2)),
        send(two_b, (0, 3)),
        send(two_c, (0, 1)),
    )


def rows_of(j):
    return pl.ds(pl.multiple_of(j * BLOCK, BLOCK), BLOCK)


def attend(i, query, cotan, key_of, add, flags, scores, tops, listed):
    pairs = len(query)
    groups = BLOCK // 8
    wide = 2 * BLOCK
    key_at = lax.broadcasted_iota(jnp.int32, (BLOCK, wide), 0)
    query_at = lax.rem(lax.broadcasted_iota(jnp.int32, (BLOCK, wide), 1), BLOCK)

    def collect(j, found):
        listed[found] = j
        return found + flags[i, j]

    listed[0] = i
    found = lax.fori_loop(0, i, collect, 1)

    def absorb(slots, p, blocks, top, total):
        newer = top
        for block in blocks:
            newer = jnp.maximum(newer, jnp.max(block, axis=0))
        total = total * jnp.exp(top - newer)
        for n, block in zip(slots, blocks):
            block = jnp.exp(block - newer[None])
            scores[p, n] = block
            tops[p, n] = newer
            total = total + jnp.sum(block, axis=0)
        return newer, total

    def raw(n, p):
        return mm(key_of(listed[n], p), query[p], 1, 1).reshape(groups, 8, wide)

    held = []
    for p in range(pairs):
        own = mm(key_of(i, p), query[p], 1, 1)
        own = jnp.where(key_at <= query_at, own, NEG).reshape(groups, 8, wide)
        floor = jnp.full((8, wide), NEG, F32)
        held.append(absorb((0,), p, (own,), floor, jnp.zeros((8, wide), F32)))

    def first(unroll, start):
        def step(n, held):
            slots = [start + unroll * n + m for m in range(unroll)]
            blocks = [[raw(n, p) for n in slots] for p in range(pairs)]
            return tuple(absorb(slots, p, blocks[p], *held[p]) for p in range(pairs))

        return step

    held, done = tuple(held), 1
    for unroll in UNROLLS[pairs]:
        turns = (found - done) // unroll
        held = lax.fori_loop(0, turns, first(unroll, done), held)
        done = done + unroll * turns
    highest, share = [], []
    for top, total in held:
        most = jnp.max(top, axis=0, keepdims=True)
        total = jnp.sum(total * jnp.exp(top - most), axis=0, keepdims=True)
        highest.append(most)
        share.append(1.0 / total)

    def second(unroll, start):
        def step(n, _):
            parts = []
            for slot in [start + unroll * n + m for m in range(unroll)]:
                for p in range(pairs):
                    factor = jnp.exp(tops[p, slot] - highest[p]) * share[p]
                    block = (scores[p, slot] * factor[None]).reshape(BLOCK, wide).astype(BF)
                    parts.append((slot, p, mm(block, cotan[p], 1, 0)))
            for slot, p, part in parts:
                add(listed[slot], p, part)
            return 0

        return step

    done = 0
    for unroll in UNROLLS[pairs]:
        turns = (found - done) // unroll
        lax.fori_loop(0, turns, second(unroll, done), 0)
        done = done + unroll * turns


def soft_quad_kernel(root, z_ref, flags, q_ref, k_ref, u_ref, three, key_all, key_c, key_d, two_a, two_b, key_two, *refs):
    outs, (queries, keys, cotans, summed, near, summed_near, scores, tops, listed) = refs[:8], refs[8:]
    wide, three_d, three_e, three_f, out_a, out_b, out_c, mine = outs
    rows = q_ref.shape[0]
    per = rows // BLOCK
    z = z_ref[0]
    root = jnp.asarray(root, BF)
    summed[...] = jnp.zeros_like(summed)

    def part(n):
        return slice(n * rows, (n + 1) * rows)

    def lanes(p):
        return slice(p * BLOCK, (p + 1) * BLOCK)

    def place(n, q, k, u, width):
        queries[part(n), :width] = q * root
        keys[part(2 + n), :width] = k
        cotans[part(n), :width] = u

    for me in range(4):

        @pl.when(z == me)
        def _(me=me):
            if me == 1:
                near[part(0), :] = key_all[...]
                near[part(1), :] = k_ref[...]
                return
            pairs = len(OWNED[me])
            width = pairs * BLOCK
            own = slice(OWNED[me][0] * BLOCK, (OWNED[me][0] + pairs) * BLOCK)
            if me == 0:
                place(0, two_a[0], two_a[1], two_a[2], width)
                place(1, two_b[0], two_b[1], two_b[2], width)
                keys[part(0), :width] = k_ref[:, own]
                keys[part(1), :width] = key_two[...]
                near[part(0), :] = k_ref[...]
            else:
                place(me - 2, q_ref[:, own], k_ref[:, own], u_ref[:, own], width)
                place(3 - me, three[0], three[1], three[2], width)
                keys[part(0), :width] = (key_c if me == 2 else key_d)[...]
                keys[part(1), :width] = (key_d if me == 2 else key_c)[...]

    def far_rows(pairs):
        def query_block(n, _):
            at = rows_of(n)

            def add(j, p, x):
                summed[rows_of(j), lanes(p)] += x

            attend(
                n + 2 * per,
                [split_pair(queries[at, lanes(p)]) for p in range(pairs)],
                [split_pair(cotans[at, lanes(p)]) for p in range(pairs)],
                lambda j, p: keys[rows_of(j), lanes(p)],
                add, flags, scores, tops, listed,
            )
            return 0

        lax.fori_loop(0, 2 * per, query_block, 0)

    @pl.when(z >= 2)
    def _():
        far_rows(3)

    @pl.when(z == 0)
    def _():
        far_rows(2)

    @pl.when(z < 2)
    def _():
        summed_near[...] = jnp.zeros_like(summed_near)

        def near_block(n, _):
            group, block = n // per, lax.rem(n, per)
            at = rows_of(block)

            def side(p):
                return pl.ds(pl.multiple_of((8 * group + p) * BLOCK, BLOCK), BLOCK)

            def add(j, p, x):
                summed_near[rows_of(j), side(p)] += x

            attend(
                block + z * per,
                [split_pair(q_ref[at, side(p)] * root) for p in range(8)],
                [split_pair(u_ref[at, side(p)]) for p in range(8)],
                lambda j, p: near[rows_of(j), side(p)],
                add, flags, scores, tops, listed,
            )
            return 0

        lax.fori_loop(0, per * (SHARE // 8), near_block, 0)

    for me in range(4):

        @pl.when(z == me)
        def _(me=me):
            if me == 1:
                wide[...] = summed_near[part(0), :].astype(BF)
                mine[...] = summed_near[part(1), :]
                return
            pairs = len(OWNED[me])
            width = pairs * BLOCK
            own = slice(OWNED[me][0] * BLOCK, (OWNED[me][0] + pairs) * BLOCK)
            if me == 0:
                out_c[...] = summed[part(1), :width].astype(BF)
                out_a[...] = summed[part(2), :width].astype(BF)
                out_b[...] = summed[part(3), :width].astype(BF)
                mine[...] = summed_near[part(0), :]
                mine[:, own] += summed[part(0), :width]
            else:
                three_d[...] = summed[part(me - 2), :].astype(BF)
                three_e[...] = summed[part(3 - me), :].astype(BF)
                three_f[...] = summed[part(5 - me), :].astype(BF)
                mine[:, own] = summed[part(me), :]


def soft_quad(here, flags, arrays, pieces, root, chunk):
    rows = arrays[0].shape[0]
    span = 4 * rows

    def whole(shape):
        return pl.BlockSpec(shape, lambda i, z, f, n=len(shape): (0,) * n, pipeline_mode=pl.Buffered(1))

    column = pl.BlockSpec((rows, SHARE * BLOCK), lambda i, z, f: (0, chunk), pipeline_mode=pl.Buffered(1))
    shapes = [(rows, SHARE * BLOCK)] + [(rows, 3 * BLOCK)] * 3 + [(rows, 2 * BLOCK)] * 3 + [(rows, SHARE * BLOCK)]
    return pl.pallas_call(
        functools.partial(soft_quad_kernel, root),
        out_shape=[jax.ShapeDtypeStruct(shape, BF) for shape in shapes[:-1]]
        + [jax.ShapeDtypeStruct(shapes[-1], F32)],
        grid_spec=pltpu.PrefetchScalarGridSpec(
            num_scalar_prefetch=2,
            grid=(1,),
            in_specs=[column] * 3 + [whole(piece.shape) for piece in pieces],
            out_specs=[whole(shape) for shape in shapes],
            scratch_shapes=[
                pltpu.VMEM((2 * rows, 3 * BLOCK), BF),
                pltpu.VMEM((span, 3 * BLOCK), BF),
                pltpu.VMEM((2 * rows, 3 * BLOCK), BF),
                pltpu.VMEM((span, 3 * BLOCK), F32),
                pltpu.VMEM((2 * rows, SHARE * BLOCK), BF),
                pltpu.VMEM((2 * rows, SHARE * BLOCK), F32),
                pltpu.VMEM((8, span // BLOCK, BLOCK // 8, 8, 2 * BLOCK), F32),
                pltpu.VMEM((8, span // BLOCK, 8, 2 * BLOCK), F32),
                pltpu.SMEM((span // BLOCK + 1,), jnp.int32),
            ],
        ),
        compiler_params=params(56),
        cost_estimate=pl.CostEstimate(
            flops=8 * span * span * BLOCK, transcendentals=2 * span * span, bytes_accessed=64 * span * BLOCK
        ),
        name="soft",
    )(here, flags, *arrays, *pieces)


def merge_kernel(z_ref, mine, wide, three_d, three_e, three_f, two_a, two_b, two_c, lit_ref):
    z = z_ref[0]
    first = slice(0, 2 * BLOCK)
    third, fourth = slice(2 * BLOCK, 5 * BLOCK), slice(5 * BLOCK, 8 * BLOCK)

    def plus(at, x):
        lit_ref[:, at] = (mine[:, at] + x.astype(F32)).astype(BF)

    def keep(at):
        lit_ref[:, at] = mine[:, at].astype(BF)

    @pl.when(z == 0)
    def _():
        plus(first, wide[:, first])
        plus(third, wide[:, third].astype(F32) + three_d[...].astype(F32))
        plus(fourth, wide[:, fourth].astype(F32) + three_e[...].astype(F32))

    @pl.when(z == 1)
    def _():
        plus(first, two_c[...])
        plus(third, three_e[...])
        plus(fourth, three_d[...])

    @pl.when(z == 2)
    def _():
        lit_ref[:, first] = two_a[...]
        keep(third)
        lit_ref[:, fourth] = three_f[...]

    @pl.when(z == 3)
    def _():
        lit_ref[:, first] = two_b[...]
        lit_ref[:, third] = three_f[...]
        keep(fourth)


def merge(here, mine, pieces):
    vmem = pl.BlockSpec(memory_space=pltpu.VMEM)
    return pl.pallas_call(
        merge_kernel,
        out_shape=jax.ShapeDtypeStruct(mine.shape, BF),
        in_specs=[pl.BlockSpec(memory_space=pltpu.SMEM)] + [vmem] * 8,
        out_specs=vmem,
        compiler_params=params(24),
        cost_estimate=pl.CostEstimate(flops=4 * mine.size, transcendentals=0, bytes_accessed=10 * mine.size),
        name="merge",
    )(here, mine, *pieces)


def triangle():
    row = lax.broadcasted_iota(jnp.int32, (BLOCK, BLOCK), 0)
    column = lax.broadcasted_iota(jnp.int32, (BLOCK, BLOCK), 1)
    return row >= column


def spread_decays(decays, first, width, each):
    heads = decays.shape[1]
    head = lax.broadcasted_iota(jnp.int32, (heads, width), 0)
    lane = lax.broadcasted_iota(jnp.int32, (heads, width), 1)
    spread = (head == first + lane // each).astype(F32).astype(BF)
    return mm(decays, spread, 1, 0).astype(BF)


def device_levels(decays, first, width):
    wide = spread_decays(decays, first, width, BLOCK // 2)
    lower = triangle().astype(F32).astype(BF)
    before = jnp.zeros((1, width), F32)
    levels = []
    for b in range(decays.shape[0] // BLOCK):
        level = mm(lower, wide[b * BLOCK : (b + 1) * BLOCK], 1, 0)
        levels.append(level + before)
        before = before + level[BLOCK - 1 :]
    return jnp.concatenate(levels, axis=0), before


def by_lane(first, second):
    lane = lax.broadcasted_iota(jnp.int32, first.shape, 1)
    return jnp.where(lane < BLOCK // 2, first, second)


def on_diagonal(x):
    row = lax.broadcasted_iota(jnp.int32, x.shape, 0)
    lane = lax.broadcasted_iota(jnp.int32, x.shape, 1)
    half = BLOCK // 2
    return jnp.where((row < half) == (lane < half), x, 0.0)


def fold(x):
    return x[: BLOCK // 2] + x[BLOCK // 2 :]


def state_kernel(q_ref, k_ref, v_ref, d_ref, sum_ref, total_ref, scaled_ref):
    level, last = device_levels(d_ref[...], 2 * pl.program_id(0), BLOCK)
    key = (k_ref[...].astype(F32) * jnp.exp(level - last)).astype(BF)
    sum_ref[0] = fold(on_diagonal(mm(key, v_ref[...], 0, 0))).astype(BF)
    thirds, rest = [], last
    for _ in range(3):
        thirds.append(rest.astype(BF))
        rest = rest - thirds[-1].astype(F32)
    blank = jnp.zeros((total_ref.shape[1] - 3, BLOCK), BF)
    total_ref[0] = jnp.concatenate(thirds + [blank], axis=0)
    scaled_ref[...] = (q_ref[...].astype(F32) * jnp.exp(-level)).astype(BF)


def device_state(light_query, light_key, light_value, decays, pairs):
    rows = light_key.shape[0]
    block = pl.BlockSpec((rows, BLOCK), lambda p: (0, p))
    return pl.pallas_call(
        state_kernel,
        out_shape=[
            jax.ShapeDtypeStruct((pairs, BLOCK // 2, BLOCK), BF),
            jax.ShapeDtypeStruct((pairs, 8, BLOCK), BF),
            jax.ShapeDtypeStruct(light_query.shape, BF),
        ],
        grid=(pairs,),
        in_specs=[block, block, block, pl.BlockSpec(decays.shape, lambda p: (0, 0))],
        out_specs=[
            pl.BlockSpec((1, BLOCK // 2, BLOCK), lambda p: (p, 0, 0)),
            pl.BlockSpec((1, 8, BLOCK), lambda p: (p, 0, 0)),
            block,
        ],
        compiler_params=params(60),
        cost_estimate=pl.CostEstimate(
            flops=8 * rows * pairs * BLOCK * BLOCK, transcendentals=rows * pairs * BLOCK, bytes_accessed=8 * rows * pairs * BLOCK
        ),
        name="state",
    )(light_query, light_key, light_value, decays)


def take_lit(count, z, lits, held):
    @pl.when(pl.program_id(0) == 0)
    def _():
        per = lits[0].shape[1] // BLOCK
        for k in range(count):
            owner = lax.rem(z - k + count, count)
            for p in range(per):
                held[owner * per + p] = lits[k][:, p * BLOCK : (p + 1) * BLOCK]


def reach_kernel(count, z_ref, q_ref, *refs):
    lits, sum_ref = refs[:count], refs[count]
    _, width = lits[0].shape
    per = width // BLOCK
    for k in range(count):
        owner = lax.rem(z_ref[0] - k + count, count)
        for p in range(per):
            at = pl.ds(pl.multiple_of((owner * per + p) * BLOCK, BLOCK), BLOCK)
            product = mm(q_ref[:, at], lits[k][:, p * BLOCK : (p + 1) * BLOCK], 0, 0)
            sum_ref[owner * per + p] = fold(on_diagonal(product)).astype(BF)


def device_reach(here, scaled, lits, chunk):
    count = len(lits)
    rows, width = lits[0].shape
    pairs = count * width // BLOCK
    return pl.pallas_call(
        functools.partial(reach_kernel, count),
        out_shape=jax.ShapeDtypeStruct((pairs, BLOCK // 2, BLOCK), BF),
        grid_spec=pltpu.PrefetchScalarGridSpec(
            num_scalar_prefetch=1,
            grid=(1,),
            in_specs=[pl.BlockSpec((rows, count * width), lambda p, z: (0, chunk))]
            + [pl.BlockSpec((rows, width), lambda p, z: (0, 0))] * count,
            out_specs=pl.BlockSpec((pairs, BLOCK // 2, BLOCK), lambda p, z: (0, 0, 0)),
        ),
        compiler_params=params(),
        cost_estimate=pl.CostEstimate(
            flops=2 * rows * pairs * BLOCK * BLOCK, transcendentals=0, bytes_accessed=4 * rows * pairs * BLOCK
        ),
        name="reach",
    )(here, scaled, *lits)


def chain_kernel(x_ref, a_ref, o_ref):
    count, half = x_ref.shape[0], x_ref.shape[1] // 2
    zero = jnp.zeros((half, x_ref.shape[2]), F32)

    def step(n, carried):
        early, late = carried
        m = count - 1 - n
        o_ref[n, :half, :] = early.astype(BF)
        o_ref[m, half:, :] = late.astype(BF)
        early = a_ref[n] * early + x_ref[n, :half, :].astype(F32)
        late = a_ref[m] * late + x_ref[m, half:, :].astype(F32)
        return early, late

    lax.fori_loop(0, count, step, (zero, zero))


def chain(items, totals):
    vmem = pl.BlockSpec(memory_space=pltpu.VMEM)
    return pl.pallas_call(
        chain_kernel,
        out_shape=jax.ShapeDtypeStruct(items.shape, BF),
        in_specs=[vmem, vmem],
        out_specs=vmem,
        compiler_params=params(),
        cost_estimate=pl.CostEstimate(flops=2 * items.size, transcendentals=0, bytes_accessed=8 * items.size),
        name="chain",
    )(items, totals)


def local_kernel(count, first_pair, skip, olds, z_ref, q_ref, k_ref, v_ref, d_ref, *refs):
    lits = refs[:count]
    gq_ref, gk_ref, gv_ref, lit_ref, held = refs[count + olds :]
    take_lit(count, z_ref[0], lits, held)
    here = pl.program_id(0)
    blocks = q_ref.shape[0] // BLOCK
    shape = (BLOCK, BLOCK)
    row_at = lax.broadcasted_iota(jnp.int32, shape, 0)
    lane_at = lax.broadcasted_iota(jnp.int32, shape, 1)
    lower, upper = row_at >= lane_at, row_at <= lane_at
    ones_lower, ones_upper = (side.astype(F32).astype(BF) for side in (lower, upper))
    slot = skip + here
    spread = spread_decays(d_ref[...], 2 * (first_pair + slot), 2 * BLOCK, BLOCK)
    heads = d_ref.shape[1]
    picked = lax.broadcasted_iota(jnp.int32, (8, heads), 1) - 2 * (first_pair + slot)
    picked = picked == lax.broadcasted_iota(jnp.int32, (8, heads), 0) // 4
    lines = mm(picked.astype(F32).astype(BF), d_ref[...], 1, 1).astype(BF)
    lit_ref[...] = held[slot]
    state = None
    kept = []
    for b in range(blocks):
        at = slice(b * BLOCK, (b + 1) * BLOCK)
        query, key, value, lit = (q_ref[at, :], k_ref[at, :], v_ref[at, :], held[slot, at, :])
        levels = mm(ones_lower, spread[at], 1, 0)
        lined = mm(lines[:, at], ones_upper, 1, 0)
        columns = (levels[:, :BLOCK], levels[:, BLOCK:])
        level = by_lane(*columns)
        last = level[BLOCK - 1 :]
        entries = jnp.exp(-level)
        leaving = jnp.exp(level - last)
        decay = jnp.exp(-last)
        spans = [lined[4 * n : 4 * n + 1] - columns[n] for n in range(2)]
        weights = jnp.concatenate(
            [jnp.where(lower, jnp.exp(jnp.minimum(span, 0.0)), 0.0) for span in spans], axis=1
        )
        turned = jnp.concatenate(
            [jnp.where(upper, jnp.exp(jnp.minimum(-span, 0.0)), 0.0) for span in spans], axis=1
        )
        queries, keys, values, twice = (split_pair(query), split_pair(key), split_pair(value), split_pair(lit))
        back = (mm(lit, values, 1, 1) * weights).astype(BF)
        back_turned = (mm(value, twice, 1, 1) * turned).astype(BF)
        mixed_turned = (mm(key, queries, 1, 1) * turned).astype(BF)
        grad_query = mm(back, keys, 1, 0)
        if state is not None:
            grad_query = grad_query + entries * mm(lit, state.astype(BF), 1, 1)
        gq_ref[at, :] = grad_query
        grad_key = mm(back_turned, queries, 1, 0)
        grad_value = mm(mixed_turned, twice, 1, 0)
        kept.append((grad_key, grad_value, entries, leaving, decay))
        if b < blocks - 1:
            left = (key.astype(F32) * leaving).astype(BF)
            left = on_diagonal(mm(left, value, 0, 0))
            state = left if state is None else decay * state + left
    state = None
    for b in reversed(range(blocks)):
        at = slice(b * BLOCK, (b + 1) * BLOCK)
        grad_key, grad_value, entries, leaving, decay = kept[b]
        if state is not None:
            low = state.astype(BF)
            grad_key = grad_key + leaving * mm(v_ref[at, :], low, 1, 1)
            grad_value = grad_value + leaving * mm(k_ref[at, :], low, 1, 0)
        gk_ref[at, :] = grad_key
        gv_ref[at, :] = grad_value
        if b > 0:
            query = (q_ref[at, :].astype(F32) * entries).astype(BF)
            query = on_diagonal(mm(query, held[slot, at, :], 0, 0))
            state = query if state is None else decay * state + query


def local(here, light_query, light_key, light_value, decays, lits, first, skip, many, olds):
    count = len(lits)
    rows, columns = light_query.shape
    width = lits[0].shape[1]
    pairs = count * width // BLOCK
    block = pl.BlockSpec((rows, BLOCK), lambda p, z: (0, first + skip + p))
    base = 5 + count
    return pl.pallas_call(
        functools.partial(local_kernel, count, first, skip, len(olds)),
        out_shape=[jax.ShapeDtypeStruct((rows, columns), F32)] * 3 + [jax.ShapeDtypeStruct((rows, columns), BF)],
        grid_spec=pltpu.PrefetchScalarGridSpec(
            num_scalar_prefetch=1,
            grid=(many,),
            in_specs=[
                block,
                block,
                block,
                pl.BlockSpec(decays.shape, lambda p, z: (0, 0)),
            ]
            + [pl.BlockSpec((rows, width), lambda p, z: (0, 0))] * count
            + [pl.BlockSpec(memory_space=pl.ANY)] * len(olds),
            out_specs=[block] * 4,
            scratch_shapes=[pltpu.VMEM((pairs, rows, BLOCK), BF)],
        ),
        input_output_aliases={base + n: n for n in range(len(olds))},
        compiler_params=params(60),
        cost_estimate=pl.CostEstimate(
            flops=40 * rows * many * BLOCK * BLOCK, transcendentals=4 * rows * many * BLOCK, bytes_accessed=22 * rows * many * BLOCK
        ),
        name="local",
    )(here, light_query, light_key, light_value, decays, *lits, *olds)


def wide_state(x):
    pairs = x.shape[0]
    width = pairs * BLOCK
    x = jnp.concatenate([x[p] for p in range(pairs)], axis=1)
    x = jnp.concatenate([x] * (2 * pairs), axis=0)
    half = BLOCK // 2
    row = lax.broadcasted_iota(jnp.int32, (width, width), 0) // half
    lane = lax.broadcasted_iota(jnp.int32, (width, width), 1) // half
    return x * (row == lane).astype(F32).astype(BF)


def final_kernel(scale, pq_ref, pk_ref, pv_ref, lit_ref, k_ref, v_ref, d_ref, s_ref, r_ref, gq_ref, gk_ref, gv_ref):
    pairs = s_ref.shape[0]
    width = pairs * BLOCK
    level, last = device_levels(d_ref[...], 2 * pairs * pl.program_id(0), width)
    entries = scale * jnp.exp(-level)
    leaving = scale * jnp.exp(level - last)
    state, reach = wide_state(s_ref[...]), wide_state(r_ref[...])
    gq_ref[...] = (scale * pq_ref[...] + entries * mm(lit_ref[...], state, 1, 1)).astype(BF)
    gk_ref[...] = (scale * pk_ref[...] + leaving * mm(v_ref[...], reach, 1, 1)).astype(BF)
    gv_ref[...] = (scale * pv_ref[...] + leaving * mm(k_ref[...], reach, 1, 0)).astype(BF)


def final(parts, light_key, light_value, decays, state_in, reach_in, scale):
    rows, columns = light_key.shape
    pairs = columns // BLOCK
    step = 2 if pairs % 2 == 0 else 1
    block = pl.BlockSpec((rows, step * BLOCK), lambda p: (0, p))
    small = pl.BlockSpec((step, BLOCK // 2, BLOCK), lambda p: (p, 0, 0))
    return pl.pallas_call(
        functools.partial(final_kernel, scale),
        out_shape=[jax.ShapeDtypeStruct((rows, columns), BF)] * 3,
        grid=(pairs // step,),
        in_specs=[block] * 6 + [pl.BlockSpec(decays.shape, lambda p: (0, 0)), small, small],
        out_specs=[block] * 3,
        compiler_params=params(60),
        cost_estimate=pl.CostEstimate(
            flops=6 * rows * columns * BLOCK, transcendentals=2 * rows * columns, bytes_accessed=24 * rows * columns
        ),
        name="final",
    )(*parts, light_key, light_value, decays, state_in, reach_in)


def turn(pieces, count):
    return [pieces[0]] + [
        lax.ppermute(pieces[k], "head", [(i, (i + k) % count) for i in range(count)])
        for k in range(1, count)
    ]


def program(light_query, light_key, light_value, soft_query, soft_key, upstream, decays, block_mask):
    count, spans = lax.axis_size("head"), lax.axis_size("ctx")
    devices = count * spans
    _, columns = light_query.shape
    heads = decays.shape[1]
    head_width = columns // heads
    pairs = heads // 2
    share = pairs // count
    chunks = 2 if share % 2 == 0 else 1
    per = share // chunks
    assert 2 * head_width == BLOCK and share * count == pairs
    part = count * per * head_width // devices
    again = head_width // part
    assert part * again == head_width
    scale = 1.0 / (head_width * math.sqrt(head_width))
    root = 1.0 / math.sqrt(head_width)
    here = lax.axis_index("head").astype(jnp.int32).reshape(1)

    arrays = (soft_query, soft_key, upstream)
    quad = count == 4 and chunks * SHARE == pairs
    packed = []
    for c in range(chunks):
        if quad:
            pieces = pack_quad(here, arrays, c)
        else:
            pieces = pack(here, arrays, c, count, per * BLOCK)
        packed.append(turn_in(pieces) if quad else turn(pieces, count))
    sums, totals, scaled = device_state(light_query, light_key, light_value, decays, pairs)

    parts, reaches = (), []
    for c in range(chunks):
        if quad:
            *lits, mine = soft_quad(here, block_mask, arrays, packed[c], root, c)
        else:
            lits = soft(here, block_mask, packed[c], root)
        lits = turn_out(lits) if quad else turn(lits, count)
        if quad:
            lits = (merge(here, mine, lits),)
        reaches.append(device_reach(here, scaled, lits, c))
        first, many = c * count * per, count * per
        cuts = (0, many // 2, many) if c == chunks - 1 else (0, many)
        for n in range(len(cuts) - 1):
            parts = local(
                here, light_query, light_key, light_value, decays, lits, first,
                cuts[n], cuts[n + 1] - cuts[n], tuple(parts),
            )

    def exchange(x):
        return lax.all_to_all(x, AXES, split_axis=0, concat_axis=0, tiled=True)

    def spread(x):
        x = x.reshape(chunks, devices, part, BLOCK)
        return jnp.swapaxes(x, 0, 1).reshape(devices, chunks * part, BLOCK)

    def gather(x):
        x = x.reshape(devices, chunks, part, BLOCK)
        return jnp.swapaxes(x, 0, 1).reshape(pairs, head_width, BLOCK)

    thirds = jnp.transpose(totals[:, :3].reshape(chunks, count * per, 3, BLOCK), (1, 2, 0, 3))
    thirds = jnp.repeat(thirds.reshape(count * per, 3 * chunks, BLOCK), again, axis=0)
    half = chunks * part
    fill = jnp.zeros((devices, -(2 * half + 3 * chunks) % 8, BLOCK), BF)
    sends = [spread(sums), spread(jnp.concatenate(reaches, axis=0)), thirds, fill]
    got = exchange(jnp.concatenate(sends, axis=1))
    thirds = got[:, 2 * half : 2 * half + 3 * chunks].astype(F32).reshape(devices, 3, chunks, BLOCK)
    rates = jnp.exp(-(thirds[:, 0] + thirds[:, 1] + thirds[:, 2]))
    rates = jnp.repeat(rates, part, axis=1)
    given = chain(got[:, : 2 * half], rates)
    given = exchange(given)
    return tuple(
        final(parts, light_key, light_value, decays, gather(given[:, :half]), gather(given[:, half:]), scale)
    )


def solution(mesh):
    rows = P(AXES, None)
    return jax.shard_map(
        program,
        mesh=mesh,
        in_specs=(rows,) * 7 + (P("ctx", None),),
        out_specs=(rows,) * 3,
        check_vma=False,
    )
```

```python
import functools
import math

import jax
import jax.numpy as jnp
from jax import lax
from jax.experimental import pallas as pl
from jax.experimental.pallas import tpu as pltpu
from jax.sharding import PartitionSpec as P


BLOCK = 128
BF = jnp.bfloat16
F32 = jnp.float32
NEG = -1e30
AXES = ("ctx", "head")


def mm(a, b, ca, cb):
    return lax.dot_general(a, b, (((ca,), (cb,)), ((), ())), preferred_element_type=F32)


def params(megabytes=48):
    return pltpu.CompilerParams(vmem_limit_bytes=megabytes * 2**20)


def lane_masks(width):
    lane = lax.broadcasted_iota(jnp.int32, (1, width), 1)
    left = (lane < width // 2).astype(F32).astype(BF)
    right = (lane >= width // 2).astype(F32).astype(BF)
    return left, right


def split_pair(x):
    left, right = lane_masks(x.shape[1])
    return jnp.concatenate([x * left, x * right], axis=0)


def pack_kernel(count, _, *refs):
    ins, outs = refs[: 3 * count], refs[3 * count :]
    for k in range(count):
        for n in range(3):
            outs[k][n] = ins[3 * k + n][...]


def pack(here, arrays, chunk, count, width):
    rows = arrays[0].shape[0]

    def spec(k):
        return pl.BlockSpec(
            (rows, width), lambda i, z: (0, chunk * count + lax.rem(z[0] + k, count))
        )

    return pl.pallas_call(
        functools.partial(pack_kernel, count),
        out_shape=[jax.ShapeDtypeStruct((3, rows, width), BF)] * count,
        grid_spec=pltpu.PrefetchScalarGridSpec(
            num_scalar_prefetch=1,
            grid=(1,),
            in_specs=[spec(k) for k in range(count) for _ in range(3)],
            out_specs=[pl.BlockSpec((3, rows, width), lambda i, z: (0, 0, 0))] * count,
        ),
        compiler_params=params(),
        cost_estimate=pl.CostEstimate(
            flops=0, transcendentals=0, bytes_accessed=12 * count * rows * width
        ),
        name="pack",
    )(here, *(array for _ in range(count) for array in arrays))


def soft_kernel(count, root, z_ref, flags, *refs):
    ins = refs[:count]
    outs = refs[count : 2 * count]
    queries, keys, cotans, scores, tops, summed, listed = refs[2 * count :]
    rows, width = ins[0].shape[1:]
    z = z_ref[0]
    pairs = width // BLOCK
    groups = BLOCK // 8
    wide = 2 * BLOCK
    for k in range(count):
        owner = lax.rem(z - k + count, count)
        at = pl.ds(pl.multiple_of(owner * rows, rows), rows)
        queries[at, :] = ins[k][0] * jnp.asarray(root, BF)
        keys[at, :] = ins[k][1]
        cotans[at, :] = ins[k][2]
    summed[...] = jnp.zeros_like(summed)

    def rows_of(j):
        return pl.ds(pl.multiple_of(j * BLOCK, BLOCK), BLOCK)

    def lanes_of(p):
        return slice(p * BLOCK, (p + 1) * BLOCK)

    def query_block(i, _):
        query = [split_pair(queries[rows_of(i), lanes_of(p)]) for p in range(pairs)]
        cotan = [split_pair(cotans[rows_of(i), lanes_of(p)]) for p in range(pairs)]

        def collect(j, found):
            listed[found] = j
            return found + flags[i, j]

        listed[0] = i
        found = lax.fori_loop(0, i, collect, 1)
        key_at = lax.broadcasted_iota(jnp.int32, (BLOCK, wide), 0)
        query_at = lax.rem(lax.broadcasted_iota(jnp.int32, (BLOCK, wide), 1), BLOCK)

        def absorb(slots, p, blocks, top, total):
            newer = top
            for block in blocks:
                newer = jnp.maximum(newer, jnp.max(block, axis=0))
            total = total * jnp.exp(top - newer)
            for n, block in zip(slots, blocks):
                block = jnp.exp(block - newer[None])
                scores[p, n] = block
                tops[p, n] = newer
                total = total + jnp.sum(block, axis=0)
            return newer, total

        def raw(n, p):
            block = mm(keys[rows_of(listed[n]), lanes_of(p)], query[p], 1, 1)
            return block.reshape(groups, 8, wide)

        held = []
        for p in range(pairs):
            own = mm(keys[rows_of(i), lanes_of(p)], query[p], 1, 1)
            own = jnp.where(key_at <= query_at, own, NEG).reshape(groups, 8, wide)
            floor = jnp.full((8, wide), NEG, F32)
            held.append(absorb((0,), p, (own,), floor, jnp.zeros((8, wide), F32)))

        def first(unroll, start):
            def step(n, held):
                slots = [start + unroll * n + m for m in range(unroll)]
                blocks = [[raw(n, p) for n in slots] for p in range(pairs)]
                return tuple(absorb(slots, p, blocks[p], *held[p]) for p in range(pairs))

            return step

        twice = (found - 1) // 2
        held = lax.fori_loop(0, twice, first(2, 1), tuple(held))
        held = lax.fori_loop(2 * twice, found - 1, first(1, 1), held)
        highest, share = [], []
        for top, total in held:
            most = jnp.max(top, axis=0, keepdims=True)
            total = jnp.sum(total * jnp.exp(top - most), axis=0, keepdims=True)
            highest.append(most)
            share.append(1.0 / total)

        def second(unroll):
            def step(n, _):
                slots = [unroll * n + m for m in range(unroll)]
                parts = []
                for n in slots:
                    for p in range(pairs):
                        factor = jnp.exp(tops[p, n] - highest[p]) * share[p]
                        block = (scores[p, n] * factor[None]).reshape(BLOCK, wide).astype(BF)
                        parts.append((n, p, mm(block, cotan[p], 1, 0)))
                for n, p, part in parts:
                    summed[rows_of(listed[n]), lanes_of(p)] += part
                return 0

            return step

        twice = found // 2
        lax.fori_loop(0, twice, second(2), 0)
        lax.fori_loop(2 * twice, found, second(1), 0)
        return 0

    lax.fori_loop(0, count * (rows // BLOCK), query_block, 0)
    for k in range(count):
        owner = lax.rem(z + k, count)
        at = pl.ds(pl.multiple_of(owner * rows, rows), rows)
        outs[k][...] = summed[at, :].astype(BF)


def soft(here, flags, pieces, root):
    count = len(pieces)
    rows, width = pieces[0].shape[1:]
    span = count * rows
    vmem = pl.BlockSpec(memory_space=pltpu.VMEM)
    smem = pl.BlockSpec(memory_space=pltpu.SMEM)
    return pl.pallas_call(
        functools.partial(soft_kernel, count, root),
        out_shape=[jax.ShapeDtypeStruct((rows, width), BF)] * count,
        in_specs=[smem, smem] + [vmem] * count,
        out_specs=[vmem] * count,
        scratch_shapes=[
            pltpu.VMEM((span, width), BF),
            pltpu.VMEM((span, width), BF),
            pltpu.VMEM((span, width), BF),
            pltpu.VMEM((width // BLOCK, span // BLOCK, BLOCK // 8, 8, 2 * BLOCK), F32),
            pltpu.VMEM((width // BLOCK, span // BLOCK, 8, 2 * BLOCK), F32),
            pltpu.VMEM((span, width), F32),
            pltpu.SMEM((span // BLOCK + 1,), jnp.int32),
        ],
        compiler_params=params(),
        cost_estimate=pl.CostEstimate(
            flops=4 * span * span * width, transcendentals=span * span, bytes_accessed=8 * span * width
        ),
        name="soft",
    )(here, flags, *pieces)


OWNED = ((), (0, 1), (2, 3, 4), (5, 6, 7))
SHARE = 8
UNROLLS = {2: (4, 2, 1), 3: (4, 2, 1), 8: (2, 1)}


def pack_quad_kernel(z_ref, *refs):
    ins, outs = refs[:19], refs[19:]
    two, three, key_c, key_d, key_all = outs
    for n in range(3):
        two[n] = ins[n][...]
        for p in range(3):
            three[n, :, p * BLOCK : (p + 1) * BLOCK] = ins[3 + 3 * n + p][...]
        key_c[:, n * BLOCK : (n + 1) * BLOCK] = ins[12 + n][...]
        key_d[:, n * BLOCK : (n + 1) * BLOCK] = ins[15 + n][...]
    key_all[...] = ins[18][...]


def pack_quad(here, arrays, chunk):
    rows = arrays[0].shape[0]
    key = arrays[1]

    def spec(pair_of):
        return pl.BlockSpec((rows, BLOCK), lambda i, z: (0, SHARE * chunk + pair_of(z[0])))

    def far(p):
        return spec(lambda z: 5 - 3 * lax.div(z, 3) + p)

    front = pl.BlockSpec((rows, 2 * BLOCK), lambda i, z: (0, SHARE // 2 * chunk))
    operands = list(arrays) + [array for array in arrays for _ in range(3)] + [key] * 7
    specs = [front] * 3
    specs += [far(p) for p in range(3)] * 3
    specs += [spec(lambda z, p=p: 2 + 3 * jnp.minimum(z, 1) + p) for p in range(3)]
    specs += [spec(lambda z, p=p: 5 - 3 * jnp.minimum(z, 1) + p) for p in range(3)]
    specs += [pl.BlockSpec((rows, SHARE * BLOCK), lambda i, z: (0, chunk))]
    shapes = [
        (3, rows, 2 * BLOCK), (3, rows, 3 * BLOCK), (rows, 3 * BLOCK), (rows, 3 * BLOCK),
        (rows, SHARE * BLOCK),
    ]
    return pl.pallas_call(
        pack_quad_kernel,
        out_shape=[jax.ShapeDtypeStruct(shape, BF) for shape in shapes],
        grid_spec=pltpu.PrefetchScalarGridSpec(
            num_scalar_prefetch=1,
            grid=(1,),
            in_specs=specs,
            out_specs=[pl.BlockSpec(shape, lambda i, z, n=len(shape): (0,) * n) for shape in shapes],
        ),
        compiler_params=params(60),
        cost_estimate=pl.CostEstimate(flops=0, transcendentals=0, bytes_accessed=120 * rows * BLOCK),
        name="pack",
    )(here, *operands)


def send(x, *routes):
    return lax.ppermute(x, "head", routes)


def turn_in(pieces):
    two, three, key_c, key_d, key_all = pieces
    key_all = send(key_all, (0, 1))
    return (
        key_all,
        send(three, (3, 2), (2, 3)),
        send(key_c, (0, 2), (1, 3)),
        send(key_d, (0, 3), (1, 2)),
        send(two, (2, 1)),
        send(two, (3, 1)),
    )


def turn_out(pieces):
    three_d, three_e, three_f, two_a, two_b, two_c = pieces
    return (
        send(three_d, (2, 0), (3, 1)),
        send(three_e, (2, 1), (3, 0)),
        send(three_f, (2, 3), (3, 2)),
        send(two_a, (1, 2)),
        send(two_b, (1, 3)),
        send(two_c, (1, 0)),
    )


def rows_of(j):
    return pl.ds(pl.multiple_of(j * BLOCK, BLOCK), BLOCK)


def attend(i, query, cotan, key_of, add, flags, scores, tops, listed):
    pairs = len(query)
    groups = BLOCK // 8
    wide = 2 * BLOCK
    key_at = lax.broadcasted_iota(jnp.int32, (BLOCK, wide), 0)
    query_at = lax.rem(lax.broadcasted_iota(jnp.int32, (BLOCK, wide), 1), BLOCK)

    def collect(j, found):
        listed[found] = j
        return found + flags[i, j]

    listed[0] = i
    found = lax.fori_loop(0, i, collect, 1)

    def absorb(slots, p, blocks, top, total):
        newer = top
        for block in blocks:
            newer = jnp.maximum(newer, jnp.max(block, axis=0))
        total = total * jnp.exp(top - newer)
        for n, block in zip(slots, blocks):
            block = jnp.exp(block - newer[None])
            scores[p, n] = block
            tops[p, n] = newer
            total = total + jnp.sum(block, axis=0)
        return newer, total

    def raw(n, p):
        return mm(key_of(listed[n], p), query[p], 1, 1).reshape(groups, 8, wide)

    held = []
    for p in range(pairs):
        own = mm(key_of(i, p), query[p], 1, 1)
        own = jnp.where(key_at <= query_at, own, NEG).reshape(groups, 8, wide)
        floor = jnp.full((8, wide), NEG, F32)
        held.append(absorb((0,), p, (own,), floor, jnp.zeros((8, wide), F32)))

    def first(unroll, start):
        def step(n, held):
            slots = [start + unroll * n + m for m in range(unroll)]
            blocks = [[raw(n, p) for n in slots] for p in range(pairs)]
            return tuple(absorb(slots, p, blocks[p], *held[p]) for p in range(pairs))

        return step

    held, done = tuple(held), 1
    for unroll in UNROLLS[pairs]:
        turns = (found - done) // unroll
        held = lax.fori_loop(0, turns, first(unroll, done), held)
        done = done + unroll * turns
    highest, share = [], []
    for top, total in held:
        most = jnp.max(top, axis=0, keepdims=True)
        total = jnp.sum(total * jnp.exp(top - most), axis=0, keepdims=True)
        highest.append(most)
        share.append(1.0 / total)

    def second(unroll, start):
        def step(n, _):
            parts = []
            for slot in [start + unroll * n + m for m in range(unroll)]:
                for p in range(pairs):
                    factor = jnp.exp(tops[p, slot] - highest[p]) * share[p]
                    block = (scores[p, slot] * factor[None]).reshape(BLOCK, wide).astype(BF)
                    parts.append((slot, p, mm(block, cotan[p], 1, 0)))
            for slot, p, part in parts:
                add(listed[slot], p, part)
            return 0

        return step

    done = 0
    for unroll in UNROLLS[pairs]:
        turns = (found - done) // unroll
        lax.fori_loop(0, turns, second(unroll, done), 0)
        done = done + unroll * turns


def near_kernel(root, z_ref, flags, q_ref, k_ref, u_ref, key_all, wide, mine, near, summed, scores, tops, listed):
    rows = q_ref.shape[0]
    per = rows // BLOCK
    z = z_ref[0]
    root = jnp.asarray(root, BF)
    upper, lower = slice(0, rows), slice(rows, 2 * rows)

    @pl.when(z == 0)
    def _():
        near[upper, :] = k_ref[...]

    @pl.when(z == 1)
    def _():
        near[upper, :] = key_all[...]
        near[lower, :] = k_ref[...]

    @pl.when(z < 2)
    def _():
        summed[...] = jnp.zeros_like(summed)

        def query_block(n, _):
            at = rows_of(n)

            def side(p):
                return slice(p * BLOCK, (p + 1) * BLOCK)

            def add(j, p, x):
                summed[rows_of(j), side(p)] += x

            attend(
                n + z * per,
                [split_pair(q_ref[at, side(p)] * root) for p in range(SHARE)],
                [split_pair(u_ref[at, side(p)]) for p in range(SHARE)],
                lambda j, p: near[rows_of(j), side(p)],
                add, flags, scores, tops, listed,
            )
            return 0

        lax.fori_loop(0, per, query_block, 0)

    @pl.when(z == 0)
    def _():
        mine[...] = summed[upper, :]

    @pl.when(z == 1)
    def _():
        wide[...] = summed[upper, :].astype(BF)
        mine[...] = summed[lower, :]


def whole(shape):
    return pl.BlockSpec(shape, lambda i, z, f, n=len(shape): (0,) * n, pipeline_mode=pl.Buffered(1))


def own_columns(rows, chunk):
    return pl.BlockSpec((rows, SHARE * BLOCK), lambda i, z, f: (0, chunk), pipeline_mode=pl.Buffered(1))


def soft_near(here, flags, arrays, key_all, root, chunk):
    rows = arrays[0].shape[0]
    shape = (rows, SHARE * BLOCK)
    blocks = 2 * rows // BLOCK
    return pl.pallas_call(
        functools.partial(near_kernel, root),
        out_shape=[jax.ShapeDtypeStruct(shape, BF), jax.ShapeDtypeStruct(shape, F32)],
        grid_spec=pltpu.PrefetchScalarGridSpec(
            num_scalar_prefetch=2,
            grid=(1,),
            in_specs=[own_columns(rows, chunk)] * 3 + [whole(shape)],
            out_specs=[whole(shape)] * 2,
            scratch_shapes=[
                pltpu.VMEM((2 * rows, SHARE * BLOCK), BF),
                pltpu.VMEM((2 * rows, SHARE * BLOCK), F32),
                pltpu.VMEM((SHARE, blocks, BLOCK // 8, 8, 2 * BLOCK), F32),
                pltpu.VMEM((SHARE, blocks, 8, 2 * BLOCK), F32),
                pltpu.SMEM((blocks + 1,), jnp.int32),
            ],
        ),
        compiler_params=params(),
        cost_estimate=pl.CostEstimate(
            flops=8 * rows * rows * SHARE * BLOCK, transcendentals=2 * rows * rows * SHARE, bytes_accessed=16 * rows * SHARE * BLOCK
        ),
        name="near",
    )(here, flags, *arrays, key_all)


def far_kernel(root, z_ref, flags, q_ref, k_ref, u_ref, key_all, three, key_c, key_d, two_a, two_b, *refs):
    outs, (queries, keys, cotans, summed, scores, tops, listed) = refs[:7], refs[7:]
    three_d, three_e, three_f, out_a, out_b, out_c, mine = outs
    rows = q_ref.shape[0]
    per = rows // BLOCK
    z = z_ref[0]
    root = jnp.asarray(root, BF)

    def part(n):
        return slice(n * rows, (n + 1) * rows)

    def lanes(p):
        return slice(p * BLOCK, (p + 1) * BLOCK)

    def place(n, q, k, u, width):
        queries[part(n), :width] = q * root
        keys[part(2 + n), :width] = k
        cotans[part(n), :width] = u

    def own_of(me):
        pairs = len(OWNED[me])
        return pairs * BLOCK, slice(OWNED[me][0] * BLOCK, (OWNED[me][0] + pairs) * BLOCK)

    for me in range(1, 4):

        @pl.when(z == me)
        def _(me=me):
            width, own = own_of(me)
            if me == 1:
                place(0, two_a[0], two_a[1], two_a[2], width)
                place(1, two_b[0], two_b[1], two_b[2], width)
                keys[part(0), :width] = key_all[:, own]
                keys[part(1), :width] = k_ref[:, own]
            else:
                place(me - 2, q_ref[:, own], k_ref[:, own], u_ref[:, own], width)
                place(3 - me, three[0], three[1], three[2], width)
                keys[part(0), :width] = (key_c if me == 2 else key_d)[...]
                keys[part(1), :width] = (key_d if me == 2 else key_c)[...]

    def far_rows(pairs):
        summed[...] = jnp.zeros_like(summed)

        def query_block(n, _):
            at = rows_of(n)

            def add(j, p, x):
                summed[rows_of(j), lanes(p)] += x

            attend(
                n + 2 * per,
                [split_pair(queries[at, lanes(p)]) for p in range(pairs)],
                [split_pair(cotans[at, lanes(p)]) for p in range(pairs)],
                lambda j, p: keys[rows_of(j), lanes(p)],
                add, flags, scores, tops, listed,
            )
            return 0

        lax.fori_loop(0, 2 * per, query_block, 0)

    @pl.when(z >= 2)
    def _():
        far_rows(3)

    @pl.when(z == 1)
    def _():
        far_rows(2)

    for me in range(1, 4):

        @pl.when(z == me)
        def _(me=me):
            width, _ = own_of(me)
            mine[:, :width] = summed[part(me), :width]
            if me == 1:
                out_c[...] = summed[part(0), :width].astype(BF)
                out_a[...] = summed[part(2), :width].astype(BF)
                out_b[...] = summed[part(3), :width].astype(BF)
            else:
                three_d[...] = summed[part(me - 2), :].astype(BF)
                three_e[...] = summed[part(3 - me), :].astype(BF)
                three_f[...] = summed[part(5 - me), :].astype(BF)


def soft_far(here, flags, arrays, pieces, root, chunk):
    rows = arrays[0].shape[0]
    span = 4 * rows
    shapes = [(rows, 3 * BLOCK)] * 3 + [(rows, 2 * BLOCK)] * 3
    last = (rows, 3 * BLOCK)
    return pl.pallas_call(
        functools.partial(far_kernel, root),
        out_shape=[jax.ShapeDtypeStruct(shape, BF) for shape in shapes] + [jax.ShapeDtypeStruct(last, F32)],
        grid_spec=pltpu.PrefetchScalarGridSpec(
            num_scalar_prefetch=2,
            grid=(1,),
            in_specs=[own_columns(rows, chunk)] * 3 + [whole(piece.shape) for piece in pieces],
            out_specs=[whole(shape) for shape in shapes + [last]],
            scratch_shapes=[
                pltpu.VMEM((2 * rows, 3 * BLOCK), BF),
                pltpu.VMEM((span, 3 * BLOCK), BF),
                pltpu.VMEM((2 * rows, 3 * BLOCK), BF),
                pltpu.VMEM((span, 3 * BLOCK), F32),
                pltpu.VMEM((3, span // BLOCK, BLOCK // 8, 8, 2 * BLOCK), F32),
                pltpu.VMEM((3, span // BLOCK, 8, 2 * BLOCK), F32),
                pltpu.SMEM((span // BLOCK + 1,), jnp.int32),
            ],
        ),
        compiler_params=params(),
        cost_estimate=pl.CostEstimate(
            flops=8 * span * span * BLOCK, transcendentals=2 * span * span, bytes_accessed=64 * span * BLOCK
        ),
        name="far",
    )(here, flags, *arrays, *pieces)


def merge_kernel(z_ref, near, far, wide, three_d, three_e, three_f, two_a, two_b, two_c, lit_ref):
    z = z_ref[0]
    first = slice(0, 2 * BLOCK)
    third, fourth = slice(2 * BLOCK, 5 * BLOCK), slice(5 * BLOCK, 8 * BLOCK)

    @pl.when(z == 0)
    def _():
        for at, x in ((first, two_c), (third, three_d), (fourth, three_e)):
            lit_ref[:, at] = (near[:, at] + wide[:, at].astype(F32) + x[...].astype(F32)).astype(BF)

    @pl.when(z == 1)
    def _():
        lit_ref[:, first] = (near[:, first] + far[:, first]).astype(BF)
        lit_ref[:, third] = (near[:, third] + three_e[...].astype(F32)).astype(BF)
        lit_ref[:, fourth] = (near[:, fourth] + three_d[...].astype(F32)).astype(BF)

    @pl.when(z == 2)
    def _():
        lit_ref[:, first] = two_a[...]
        lit_ref[:, third] = far[...].astype(BF)
        lit_ref[:, fourth] = three_f[...]

    @pl.when(z == 3)
    def _():
        lit_ref[:, first] = two_b[...]
        lit_ref[:, third] = three_f[...]
        lit_ref[:, fourth] = far[...].astype(BF)


def merge(here, near, far, wide, pieces):
    vmem = pl.BlockSpec(memory_space=pltpu.VMEM)
    return pl.pallas_call(
        merge_kernel,
        out_shape=jax.ShapeDtypeStruct(near.shape, BF),
        in_specs=[pl.BlockSpec(memory_space=pltpu.SMEM)] + [vmem] * 9,
        out_specs=vmem,
        compiler_params=params(24),
        cost_estimate=pl.CostEstimate(flops=4 * near.size, transcendentals=0, bytes_accessed=10 * near.size),
        name="merge",
    )(here, near, far, wide, *pieces)


def triangle():
    row = lax.broadcasted_iota(jnp.int32, (BLOCK, BLOCK), 0)
    column = lax.broadcasted_iota(jnp.int32, (BLOCK, BLOCK), 1)
    return row >= column


def spread_decays(decays, first, width, each):
    heads = decays.shape[1]
    head = lax.broadcasted_iota(jnp.int32, (heads, width), 0)
    lane = lax.broadcasted_iota(jnp.int32, (heads, width), 1)
    spread = (head == first + lane // each).astype(F32).astype(BF)
    return mm(decays, spread, 1, 0).astype(BF)


def device_levels(decays, first, width):
    wide = spread_decays(decays, first, width, BLOCK // 2)
    lower = triangle().astype(F32).astype(BF)
    before = jnp.zeros((1, width), F32)
    levels = []
    for b in range(decays.shape[0] // BLOCK):
        level = mm(lower, wide[b * BLOCK : (b + 1) * BLOCK], 1, 0)
        levels.append(level + before)
        before = before + level[BLOCK - 1 :]
    return jnp.concatenate(levels, axis=0), before


def by_lane(first, second):
    lane = lax.broadcasted_iota(jnp.int32, first.shape, 1)
    return jnp.where(lane < BLOCK // 2, first, second)


def on_diagonal(x):
    row = lax.broadcasted_iota(jnp.int32, x.shape, 0)
    lane = lax.broadcasted_iota(jnp.int32, x.shape, 1)
    half = BLOCK // 2
    return jnp.where((row < half) == (lane < half), x, 0.0)


def fold(x):
    return x[: BLOCK // 2] + x[BLOCK // 2 :]


def state_kernel(q_ref, k_ref, v_ref, d_ref, sum_ref, total_ref, scaled_ref):
    level, last = device_levels(d_ref[...], 2 * pl.program_id(0), BLOCK)
    key = (k_ref[...].astype(F32) * jnp.exp(level - last)).astype(BF)
    sum_ref[0] = fold(on_diagonal(mm(key, v_ref[...], 0, 0))).astype(BF)
    thirds, rest = [], last
    for _ in range(3):
        thirds.append(rest.astype(BF))
        rest = rest - thirds[-1].astype(F32)
    blank = jnp.zeros((total_ref.shape[1] - 3, BLOCK), BF)
    total_ref[0] = jnp.concatenate(thirds + [blank], axis=0)
    scaled_ref[...] = (q_ref[...].astype(F32) * jnp.exp(-level)).astype(BF)


def device_state(light_query, light_key, light_value, decays, pairs):
    rows = light_key.shape[0]
    block = pl.BlockSpec((rows, BLOCK), lambda p: (0, p))
    return pl.pallas_call(
        state_kernel,
        out_shape=[
            jax.ShapeDtypeStruct((pairs, BLOCK // 2, BLOCK), BF),
            jax.ShapeDtypeStruct((pairs, 8, BLOCK), BF),
            jax.ShapeDtypeStruct(light_query.shape, BF),
        ],
        grid=(pairs,),
        in_specs=[block, block, block, pl.BlockSpec(decays.shape, lambda p: (0, 0))],
        out_specs=[
            pl.BlockSpec((1, BLOCK // 2, BLOCK), lambda p: (p, 0, 0)),
            pl.BlockSpec((1, 8, BLOCK), lambda p: (p, 0, 0)),
            block,
        ],
        compiler_params=params(60),
        cost_estimate=pl.CostEstimate(
            flops=8 * rows * pairs * BLOCK * BLOCK, transcendentals=rows * pairs * BLOCK, bytes_accessed=8 * rows * pairs * BLOCK
        ),
        name="state",
    )(light_query, light_key, light_value, decays)


def take_lit(count, z, lits, held):
    @pl.when(pl.program_id(0) == 0)
    def _():
        per = lits[0].shape[1] // BLOCK
        for k in range(count):
            owner = lax.rem(z - k + count, count)
            for p in range(per):
                held[owner * per + p] = lits[k][:, p * BLOCK : (p + 1) * BLOCK]


def reach_kernel(count, z_ref, q_ref, *refs):
    lits, sum_ref = refs[:count], refs[count]
    _, width = lits[0].shape
    per = width // BLOCK
    for k in range(count):
        owner = lax.rem(z_ref[0] - k + count, count)
        for p in range(per):
            at = pl.ds(pl.multiple_of((owner * per + p) * BLOCK, BLOCK), BLOCK)
            product = mm(q_ref[:, at], lits[k][:, p * BLOCK : (p + 1) * BLOCK], 0, 0)
            sum_ref[owner * per + p] = fold(on_diagonal(product)).astype(BF)


def device_reach(here, scaled, lits, chunk):
    count = len(lits)
    rows, width = lits[0].shape
    pairs = count * width // BLOCK
    return pl.pallas_call(
        functools.partial(reach_kernel, count),
        out_shape=jax.ShapeDtypeStruct((pairs, BLOCK // 2, BLOCK), BF),
        grid_spec=pltpu.PrefetchScalarGridSpec(
            num_scalar_prefetch=1,
            grid=(1,),
            in_specs=[pl.BlockSpec((rows, count * width), lambda p, z: (0, chunk))]
            + [pl.BlockSpec((rows, width), lambda p, z: (0, 0))] * count,
            out_specs=pl.BlockSpec((pairs, BLOCK // 2, BLOCK), lambda p, z: (0, 0, 0)),
        ),
        compiler_params=params(),
        cost_estimate=pl.CostEstimate(
            flops=2 * rows * pairs * BLOCK * BLOCK, transcendentals=0, bytes_accessed=4 * rows * pairs * BLOCK
        ),
        name="reach",
    )(here, scaled, *lits)


def chain_kernel(x_ref, a_ref, o_ref):
    count, half = x_ref.shape[0], x_ref.shape[1] // 2
    zero = jnp.zeros((half, x_ref.shape[2]), F32)

    def step(n, carried):
        early, late = carried
        m = count - 1 - n
        o_ref[n, :half, :] = early.astype(BF)
        o_ref[m, half:, :] = late.astype(BF)
        early = a_ref[n] * early + x_ref[n, :half, :].astype(F32)
        late = a_ref[m] * late + x_ref[m, half:, :].astype(F32)
        return early, late

    lax.fori_loop(0, count, step, (zero, zero))


def chain(items, totals):
    vmem = pl.BlockSpec(memory_space=pltpu.VMEM)
    return pl.pallas_call(
        chain_kernel,
        out_shape=jax.ShapeDtypeStruct(items.shape, BF),
        in_specs=[vmem, vmem],
        out_specs=vmem,
        compiler_params=params(),
        cost_estimate=pl.CostEstimate(flops=2 * items.size, transcendentals=0, bytes_accessed=8 * items.size),
        name="chain",
    )(items, totals)


def local_kernel(count, first_pair, skip, olds, z_ref, q_ref, k_ref, v_ref, d_ref, *refs):
    lits = refs[:count]
    gq_ref, gk_ref, gv_ref, lit_ref, held = refs[count + olds :]
    take_lit(count, z_ref[0], lits, held)
    here = pl.program_id(0)
    blocks = q_ref.shape[0] // BLOCK
    shape = (BLOCK, BLOCK)
    row_at = lax.broadcasted_iota(jnp.int32, shape, 0)
    lane_at = lax.broadcasted_iota(jnp.int32, shape, 1)
    lower, upper = row_at >= lane_at, row_at <= lane_at
    ones_lower, ones_upper = (side.astype(F32).astype(BF) for side in (lower, upper))
    slot = skip + here
    spread = spread_decays(d_ref[...], 2 * (first_pair + slot), 2 * BLOCK, BLOCK)
    heads = d_ref.shape[1]
    picked = lax.broadcasted_iota(jnp.int32, (8, heads), 1) - 2 * (first_pair + slot)
    picked = picked == lax.broadcasted_iota(jnp.int32, (8, heads), 0) // 4
    lines = mm(picked.astype(F32).astype(BF), d_ref[...], 1, 1).astype(BF)
    lit_ref[...] = held[slot]
    state = None
    kept = []
    for b in range(blocks):
        at = slice(b * BLOCK, (b + 1) * BLOCK)
        query, key, value, lit = (q_ref[at, :], k_ref[at, :], v_ref[at, :], held[slot, at, :])
        levels = mm(ones_lower, spread[at], 1, 0)
        lined = mm(lines[:, at], ones_upper, 1, 0)
        columns = (levels[:, :BLOCK], levels[:, BLOCK:])
        level = by_lane(*columns)
        last = level[BLOCK - 1 :]
        entries = jnp.exp(-level)
        leaving = jnp.exp(level - last)
        decay = jnp.exp(-last)
        spans = [lined[4 * n : 4 * n + 1] - columns[n] for n in range(2)]
        weights = jnp.concatenate(
            [jnp.where(lower, jnp.exp(jnp.minimum(span, 0.0)), 0.0) for span in spans], axis=1
        )
        turned = jnp.concatenate(
            [jnp.where(upper, jnp.exp(jnp.minimum(-span, 0.0)), 0.0) for span in spans], axis=1
        )
        queries, keys, values, twice = (split_pair(query), split_pair(key), split_pair(value), split_pair(lit))
        back = (mm(lit, values, 1, 1) * weights).astype(BF)
        back_turned = (mm(value, twice, 1, 1) * turned).astype(BF)
        mixed_turned = (mm(key, queries, 1, 1) * turned).astype(BF)
        grad_query = mm(back, keys, 1, 0)
        if state is not None:
            grad_query = grad_query + entries * mm(lit, state.astype(BF), 1, 1)
        gq_ref[at, :] = grad_query
        grad_key = mm(back_turned, queries, 1, 0)
        grad_value = mm(mixed_turned, twice, 1, 0)
        kept.append((grad_key, grad_value, entries, leaving, decay))
        if b < blocks - 1:
            left = (key.astype(F32) * leaving).astype(BF)
            left = on_diagonal(mm(left, value, 0, 0))
            state = left if state is None else decay * state + left
    state = None
    for b in reversed(range(blocks)):
        at = slice(b * BLOCK, (b + 1) * BLOCK)
        grad_key, grad_value, entries, leaving, decay = kept[b]
        if state is not None:
            low = state.astype(BF)
            grad_key = grad_key + leaving * mm(v_ref[at, :], low, 1, 1)
            grad_value = grad_value + leaving * mm(k_ref[at, :], low, 1, 0)
        gk_ref[at, :] = grad_key
        gv_ref[at, :] = grad_value
        if b > 0:
            query = (q_ref[at, :].astype(F32) * entries).astype(BF)
            query = on_diagonal(mm(query, held[slot, at, :], 0, 0))
            state = query if state is None else decay * state + query


def local(here, light_query, light_key, light_value, decays, lits, first, skip, many, olds):
    count = len(lits)
    rows, columns = light_query.shape
    width = lits[0].shape[1]
    pairs = count * width // BLOCK
    block = pl.BlockSpec((rows, BLOCK), lambda p, z: (0, first + skip + p))
    base = 5 + count
    return pl.pallas_call(
        functools.partial(local_kernel, count, first, skip, len(olds)),
        out_shape=[jax.ShapeDtypeStruct((rows, columns), F32)] * 3 + [jax.ShapeDtypeStruct((rows, columns), BF)],
        grid_spec=pltpu.PrefetchScalarGridSpec(
            num_scalar_prefetch=1,
            grid=(many,),
            in_specs=[
                block,
                block,
                block,
                pl.BlockSpec(decays.shape, lambda p, z: (0, 0)),
            ]
            + [pl.BlockSpec((rows, width), lambda p, z: (0, 0))] * count
            + [pl.BlockSpec(memory_space=pl.ANY)] * len(olds),
            out_specs=[block] * 4,
            scratch_shapes=[pltpu.VMEM((pairs, rows, BLOCK), BF)],
        ),
        input_output_aliases={base + n: n for n in range(len(olds))},
        compiler_params=params(60),
        cost_estimate=pl.CostEstimate(
            flops=40 * rows * many * BLOCK * BLOCK, transcendentals=4 * rows * many * BLOCK, bytes_accessed=22 * rows * many * BLOCK
        ),
        name="local",
    )(here, light_query, light_key, light_value, decays, *lits, *olds)


def wide_state(x):
    pairs = x.shape[0]
    width = pairs * BLOCK
    x = jnp.concatenate([x[p] for p in range(pairs)], axis=1)
    x = jnp.concatenate([x] * (2 * pairs), axis=0)
    half = BLOCK // 2
    row = lax.broadcasted_iota(jnp.int32, (width, width), 0) // half
    lane = lax.broadcasted_iota(jnp.int32, (width, width), 1) // half
    return x * (row == lane).astype(F32).astype(BF)


def final_kernel(scale, pq_ref, pk_ref, pv_ref, lit_ref, k_ref, v_ref, d_ref, s_ref, r_ref, gq_ref, gk_ref, gv_ref):
    pairs = s_ref.shape[0]
    width = pairs * BLOCK
    level, last = device_levels(d_ref[...], 2 * pairs * pl.program_id(0), width)
    entries = scale * jnp.exp(-level)
    leaving = scale * jnp.exp(level - last)
    state, reach = wide_state(s_ref[...]), wide_state(r_ref[...])
    gq_ref[...] = (scale * pq_ref[...] + entries * mm(lit_ref[...], state, 1, 1)).astype(BF)
    gk_ref[...] = (scale * pk_ref[...] + leaving * mm(v_ref[...], reach, 1, 1)).astype(BF)
    gv_ref[...] = (scale * pv_ref[...] + leaving * mm(k_ref[...], reach, 1, 0)).astype(BF)


def final(parts, light_key, light_value, decays, state_in, reach_in, scale):
    rows, columns = light_key.shape
    pairs = columns // BLOCK
    step = 2 if pairs % 2 == 0 else 1
    block = pl.BlockSpec((rows, step * BLOCK), lambda p: (0, p))
    small = pl.BlockSpec((step, BLOCK // 2, BLOCK), lambda p: (p, 0, 0))
    return pl.pallas_call(
        functools.partial(final_kernel, scale),
        out_shape=[jax.ShapeDtypeStruct((rows, columns), BF)] * 3,
        grid=(pairs // step,),
        in_specs=[block] * 6 + [pl.BlockSpec(decays.shape, lambda p: (0, 0)), small, small],
        out_specs=[block] * 3,
        compiler_params=params(60),
        cost_estimate=pl.CostEstimate(
            flops=6 * rows * columns * BLOCK, transcendentals=2 * rows * columns, bytes_accessed=24 * rows * columns
        ),
        name="final",
    )(*parts, light_key, light_value, decays, state_in, reach_in)


def turn(pieces, count):
    return [pieces[0]] + [
        lax.ppermute(pieces[k], "head", [(i, (i + k) % count) for i in range(count)])
        for k in range(1, count)
    ]


def program(light_query, light_key, light_value, soft_query, soft_key, upstream, decays, block_mask):
    count, spans = lax.axis_size("head"), lax.axis_size("ctx")
    devices = count * spans
    _, columns = light_query.shape
    heads = decays.shape[1]
    head_width = columns // heads
    pairs = heads // 2
    share = pairs // count
    chunks = 2 if share % 2 == 0 else 1
    per = share // chunks
    assert 2 * head_width == BLOCK and share * count == pairs
    part = count * per * head_width // devices
    again = head_width // part
    assert part * again == head_width
    scale = 1.0 / (head_width * math.sqrt(head_width))
    root = 1.0 / math.sqrt(head_width)
    here = lax.axis_index("head").astype(jnp.int32).reshape(1)

    arrays = (soft_query, soft_key, upstream)
    quad = count == 4 and chunks * SHARE == pairs
    packed = []
    for c in range(chunks):
        if quad:
            pieces = pack_quad(here, arrays, c)
        else:
            pieces = pack(here, arrays, c, count, per * BLOCK)
        packed.append(turn_in(pieces) if quad else turn(pieces, count))
    near, wide = [], []
    if quad:
        for c in range(chunks):
            sent, kept = soft_near(here, block_mask, arrays, packed[c][0], root, c)
            near.append(kept)
            wide.append(send(sent, (1, 0)))
    sums, totals, scaled = device_state(light_query, light_key, light_value, decays, pairs)

    parts, reaches = (), []
    for c in range(chunks):
        if quad:
            *lits, far = soft_far(here, block_mask, arrays, packed[c], root, c)
        else:
            lits = soft(here, block_mask, packed[c], root)
        lits = turn_out(lits) if quad else turn(lits, count)
        if quad:
            lits = (merge(here, near[c], far, wide[c], lits),)
        reaches.append(device_reach(here, scaled, lits, c))
        first, many = c * count * per, count * per
        cuts = (0, many // 2, many) if c == chunks - 1 else (0, many)
        for n in range(len(cuts) - 1):
            parts = local(
                here, light_query, light_key, light_value, decays, lits, first,
                cuts[n], cuts[n + 1] - cuts[n], tuple(parts),
            )

    def exchange(x):
        return lax.all_to_all(x, AXES, split_axis=0, concat_axis=0, tiled=True)

    def spread(x):
        x = x.reshape(chunks, devices, part, BLOCK)
        return jnp.swapaxes(x, 0, 1).reshape(devices, chunks * part, BLOCK)

    def gather(x):
        x = x.reshape(devices, chunks, part, BLOCK)
        return jnp.swapaxes(x, 0, 1).reshape(pairs, head_width, BLOCK)

    thirds = jnp.transpose(totals[:, :3].reshape(chunks, count * per, 3, BLOCK), (1, 2, 0, 3))
    thirds = jnp.repeat(thirds.reshape(count * per, 3 * chunks, BLOCK), again, axis=0)
    half = chunks * part
    fill = jnp.zeros((devices, -(2 * half + 3 * chunks) % 8, BLOCK), BF)
    sends = [spread(sums), spread(jnp.concatenate(reaches, axis=0)), thirds, fill]
    got = exchange(jnp.concatenate(sends, axis=1))
    thirds = got[:, 2 * half : 2 * half + 3 * chunks].astype(F32).reshape(devices, 3, chunks, BLOCK)
    rates = jnp.exp(-(thirds[:, 0] + thirds[:, 1] + thirds[:, 2]))
    rates = jnp.repeat(rates, part, axis=1)
    given = chain(got[:, : 2 * half], rates)
    given = exchange(given)
    return tuple(
        final(parts, light_key, light_value, decays, gather(given[:, :half]), gather(given[:, half:]), scale)
    )


def solution(mesh):
    rows = P(AXES, None)
    return jax.shard_map(
        program,
        mesh=mesh,
        in_specs=(rows,) * 7 + (P("ctx", None),),
        out_specs=(rows,) * 3,
        check_vma=False,
    )
```

```python
import functools
import math

import jax
import jax.numpy as jnp
from jax import lax
from jax.experimental import pallas as pl
from jax.experimental.pallas import tpu as pltpu
from jax.sharding import PartitionSpec as P


BLOCK = 128
BF = jnp.bfloat16
F32 = jnp.float32
NEG = -1e30
AXES = ("ctx", "head")


def mm(a, b, ca, cb):
    return lax.dot_general(a, b, (((ca,), (cb,)), ((), ())), preferred_element_type=F32)


def params(megabytes=48):
    return pltpu.CompilerParams(vmem_limit_bytes=megabytes * 2**20)


def lane_masks(width):
    lane = lax.broadcasted_iota(jnp.int32, (1, width), 1)
    left = (lane < width // 2).astype(F32).astype(BF)
    right = (lane >= width // 2).astype(F32).astype(BF)
    return left, right


def split_pair(x):
    left, right = lane_masks(x.shape[1])
    return jnp.concatenate([x * left, x * right], axis=0)


def pack_kernel(count, _, *refs):
    ins, outs = refs[: 3 * count], refs[3 * count :]
    for k in range(count):
        for n in range(3):
            outs[k][n] = ins[3 * k + n][...]


def pack(here, arrays, chunk, count, width):
    rows = arrays[0].shape[0]

    def spec(k):
        return pl.BlockSpec(
            (rows, width), lambda i, z: (0, chunk * count + lax.rem(z[0] + k, count))
        )

    return pl.pallas_call(
        functools.partial(pack_kernel, count),
        out_shape=[jax.ShapeDtypeStruct((3, rows, width), BF)] * count,
        grid_spec=pltpu.PrefetchScalarGridSpec(
            num_scalar_prefetch=1,
            grid=(1,),
            in_specs=[spec(k) for k in range(count) for _ in range(3)],
            out_specs=[pl.BlockSpec((3, rows, width), lambda i, z: (0, 0, 0))] * count,
        ),
        compiler_params=params(),
        cost_estimate=pl.CostEstimate(
            flops=0, transcendentals=0, bytes_accessed=12 * count * rows * width
        ),
        name="pack",
    )(here, *(array for _ in range(count) for array in arrays))


def soft_kernel(count, root, z_ref, flags, *refs):
    ins = refs[:count]
    outs = refs[count : 2 * count]
    queries, keys, cotans, scores, tops, summed, listed = refs[2 * count :]
    rows, width = ins[0].shape[1:]
    z = z_ref[0]
    pairs = width // BLOCK
    groups = BLOCK // 8
    wide = 2 * BLOCK
    for k in range(count):
        owner = lax.rem(z - k + count, count)
        at = pl.ds(pl.multiple_of(owner * rows, rows), rows)
        queries[at, :] = ins[k][0] * jnp.asarray(root, BF)
        keys[at, :] = ins[k][1]
        cotans[at, :] = ins[k][2]
    summed[...] = jnp.zeros_like(summed)

    def rows_of(j):
        return pl.ds(pl.multiple_of(j * BLOCK, BLOCK), BLOCK)

    def lanes_of(p):
        return slice(p * BLOCK, (p + 1) * BLOCK)

    def query_block(i, _):
        query = [split_pair(queries[rows_of(i), lanes_of(p)]) for p in range(pairs)]
        cotan = [split_pair(cotans[rows_of(i), lanes_of(p)]) for p in range(pairs)]

        def collect(j, found):
            listed[found] = j
            return found + flags[i, j]

        listed[0] = i
        found = lax.fori_loop(0, i, collect, 1)
        key_at = lax.broadcasted_iota(jnp.int32, (BLOCK, wide), 0)
        query_at = lax.rem(lax.broadcasted_iota(jnp.int32, (BLOCK, wide), 1), BLOCK)

        def absorb(slots, p, blocks, top, total):
            newer = top
            for block in blocks:
                newer = jnp.maximum(newer, jnp.max(block, axis=0))
            total = total * jnp.exp(top - newer)
            for n, block in zip(slots, blocks):
                block = jnp.exp(block - newer[None])
                scores[p, n] = block
                tops[p, n] = newer
                total = total + jnp.sum(block, axis=0)
            return newer, total

        def raw(n, p):
            block = mm(keys[rows_of(listed[n]), lanes_of(p)], query[p], 1, 1)
            return block.reshape(groups, 8, wide)

        held = []
        for p in range(pairs):
            own = mm(keys[rows_of(i), lanes_of(p)], query[p], 1, 1)
            own = jnp.where(key_at <= query_at, own, NEG).reshape(groups, 8, wide)
            floor = jnp.full((8, wide), NEG, F32)
            held.append(absorb((0,), p, (own,), floor, jnp.zeros((8, wide), F32)))

        def first(unroll, start):
            def step(n, held):
                slots = [start + unroll * n + m for m in range(unroll)]
                blocks = [[raw(n, p) for n in slots] for p in range(pairs)]
                return tuple(absorb(slots, p, blocks[p], *held[p]) for p in range(pairs))

            return step

        twice = (found - 1) // 2
        held = lax.fori_loop(0, twice, first(2, 1), tuple(held))
        held = lax.fori_loop(2 * twice, found - 1, first(1, 1), held)
        highest, share = [], []
        for top, total in held:
            most = jnp.max(top, axis=0, keepdims=True)
            total = jnp.sum(total * jnp.exp(top - most), axis=0, keepdims=True)
            highest.append(most)
            share.append(1.0 / total)

        def second(unroll):
            def step(n, _):
                slots = [unroll * n + m for m in range(unroll)]
                parts = []
                for n in slots:
                    for p in range(pairs):
                        factor = jnp.exp(tops[p, n] - highest[p]) * share[p]
                        block = (scores[p, n] * factor[None]).reshape(BLOCK, wide).astype(BF)
                        parts.append((n, p, mm(block, cotan[p], 1, 0)))
                for n, p, part in parts:
                    summed[rows_of(listed[n]), lanes_of(p)] += part
                return 0

            return step

        twice = found // 2
        lax.fori_loop(0, twice, second(2), 0)
        lax.fori_loop(2 * twice, found, second(1), 0)
        return 0

    lax.fori_loop(0, count * (rows // BLOCK), query_block, 0)
    for k in range(count):
        owner = lax.rem(z + k, count)
        at = pl.ds(pl.multiple_of(owner * rows, rows), rows)
        outs[k][...] = summed[at, :].astype(BF)


def soft(here, flags, pieces, root):
    count = len(pieces)
    rows, width = pieces[0].shape[1:]
    span = count * rows
    vmem = pl.BlockSpec(memory_space=pltpu.VMEM)
    smem = pl.BlockSpec(memory_space=pltpu.SMEM)
    return pl.pallas_call(
        functools.partial(soft_kernel, count, root),
        out_shape=[jax.ShapeDtypeStruct((rows, width), BF)] * count,
        in_specs=[smem, smem] + [vmem] * count,
        out_specs=[vmem] * count,
        scratch_shapes=[
            pltpu.VMEM((span, width), BF),
            pltpu.VMEM((span, width), BF),
            pltpu.VMEM((span, width), BF),
            pltpu.VMEM((width // BLOCK, span // BLOCK, BLOCK // 8, 8, 2 * BLOCK), F32),
            pltpu.VMEM((width // BLOCK, span // BLOCK, 8, 2 * BLOCK), F32),
            pltpu.VMEM((span, width), F32),
            pltpu.SMEM((span // BLOCK + 1,), jnp.int32),
        ],
        compiler_params=params(),
        cost_estimate=pl.CostEstimate(
            flops=4 * span * span * width, transcendentals=span * span, bytes_accessed=8 * span * width
        ),
        name="soft",
    )(here, flags, *pieces)


OWNED = ((), (0, 1), (2, 3, 4), (5, 6, 7))
SHARE = 8
IN_ORDER = (0, 1, 4, 5, 2, 3)
OUT_ORDER = (5, 3, 4, 1, 0, 2)
UNROLLS = {2: (4, 2, 1), 3: (4, 2, 1), 8: (2, 1)}


def pack_quad_kernel(z_ref, *refs):
    ins, outs = refs[:19], refs[19:]
    two, three, key_c, key_d, key_all = outs
    for n in range(3):
        two[n] = ins[n][...]
        for p in range(3):
            three[n, :, p * BLOCK : (p + 1) * BLOCK] = ins[3 + 3 * n + p][...]
        key_c[:, n * BLOCK : (n + 1) * BLOCK] = ins[12 + n][...]
        key_d[:, n * BLOCK : (n + 1) * BLOCK] = ins[15 + n][...]
    key_all[...] = ins[18][...]


def pack_quad(here, arrays, chunk):
    rows = arrays[0].shape[0]
    key = arrays[1]

    def spec(pair_of):
        return pl.BlockSpec((rows, BLOCK), lambda i, z: (0, SHARE * chunk + pair_of(z[0])))

    def far(p):
        return spec(lambda z: 5 - 3 * lax.div(z, 3) + p)

    front = pl.BlockSpec((rows, 2 * BLOCK), lambda i, z: (0, SHARE // 2 * chunk))
    operands = list(arrays) + [array for array in arrays for _ in range(3)] + [key] * 7
    specs = [front] * 3
    specs += [far(p) for p in range(3)] * 3
    specs += [spec(lambda z, p=p: 2 + 3 * jnp.minimum(z, 1) + p) for p in range(3)]
    specs += [spec(lambda z, p=p: 5 - 3 * jnp.minimum(z, 1) + p) for p in range(3)]
    specs += [pl.BlockSpec((rows, SHARE * BLOCK), lambda i, z: (0, chunk))]
    shapes = [
        (3, rows, 2 * BLOCK), (3, rows, 3 * BLOCK), (rows, 3 * BLOCK), (rows, 3 * BLOCK),
        (rows, SHARE * BLOCK),
    ]
    return pl.pallas_call(
        pack_quad_kernel,
        out_shape=[jax.ShapeDtypeStruct(shape, BF) for shape in shapes],
        grid_spec=pltpu.PrefetchScalarGridSpec(
            num_scalar_prefetch=1,
            grid=(1,),
            in_specs=specs,
            out_specs=[pl.BlockSpec(shape, lambda i, z, n=len(shape): (0,) * n) for shape in shapes],
        ),
        compiler_params=params(60),
        cost_estimate=pl.CostEstimate(flops=0, transcendentals=0, bytes_accessed=120 * rows * BLOCK),
        name="pack",
    )(here, *operands)


def send(x, *routes):
    return lax.ppermute(x, "head", routes)


def in_turn(order, jobs):
    results = [None] * len(jobs)
    for n in order:
        results[n] = send(*jobs[n])
    return tuple(results)


def turn_in(pieces):
    two, three, key_c, key_d, key_all = pieces
    jobs = (
        (key_all, (0, 1)),
        (three, (3, 2), (2, 3)),
        (key_c, (0, 2), (1, 3)),
        (key_d, (0, 3), (1, 2)),
        (two, (2, 1)),
        (two, (3, 1)),
    )
    return in_turn(IN_ORDER, jobs)


def turn_out(pieces):
    three_d, three_e, three_f, two_a, two_b, two_c = pieces
    jobs = (
        (three_d, (2, 0), (3, 1)),
        (three_e, (2, 1), (3, 0)),
        (three_f, (2, 3), (3, 2)),
        (two_a, (1, 2)),
        (two_b, (1, 3)),
        (two_c, (1, 0)),
    )
    return in_turn(OUT_ORDER, jobs)


def rows_of(j):
    return pl.ds(pl.multiple_of(j * BLOCK, BLOCK), BLOCK)


def attend(i, query, cotan, key_of, add, flags, scores, tops, listed):
    pairs = len(query)
    groups = BLOCK // 8
    wide = 2 * BLOCK
    key_at = lax.broadcasted_iota(jnp.int32, (BLOCK, wide), 0)
    query_at = lax.rem(lax.broadcasted_iota(jnp.int32, (BLOCK, wide), 1), BLOCK)

    def collect(j, found):
        listed[found] = j
        return found + flags[i, j]

    listed[0] = i
    found = lax.fori_loop(0, i, collect, 1)

    def absorb(slots, p, blocks, top, total):
        newer = top
        for block in blocks:
            newer = jnp.maximum(newer, jnp.max(block, axis=0))
        total = total * jnp.exp(top - newer)
        for n, block in zip(slots, blocks):
            block = jnp.exp(block - newer[None])
            scores[p, n] = block
            tops[p, n] = newer
            total = total + jnp.sum(block, axis=0)
        return newer, total

    def raw(n, p):
        return mm(key_of(listed[n], p), query[p], 1, 1).reshape(groups, 8, wide)

    held = []
    for p in range(pairs):
        own = mm(key_of(i, p), query[p], 1, 1)
        own = jnp.where(key_at <= query_at, own, NEG).reshape(groups, 8, wide)
        floor = jnp.full((8, wide), NEG, F32)
        held.append(absorb((0,), p, (own,), floor, jnp.zeros((8, wide), F32)))

    def first(unroll, start):
        def step(n, held):
            slots = [start + unroll * n + m for m in range(unroll)]
            blocks = [[raw(n, p) for n in slots] for p in range(pairs)]
            return tuple(absorb(slots, p, blocks[p], *held[p]) for p in range(pairs))

        return step

    held, done = tuple(held), 1
    for unroll in UNROLLS[pairs]:
        turns = (found - done) // unroll
        held = lax.fori_loop(0, turns, first(unroll, done), held)
        done = done + unroll * turns
    highest, share = [], []
    for top, total in held:
        most = jnp.max(top, axis=0, keepdims=True)
        total = jnp.sum(total * jnp.exp(top - most), axis=0, keepdims=True)
        highest.append(most)
        share.append(1.0 / total)

    def second(unroll, start):
        def step(n, _):
            parts = []
            for slot in [start + unroll * n + m for m in range(unroll)]:
                for p in range(pairs):
                    factor = jnp.exp(tops[p, slot] - highest[p]) * share[p]
                    block = (scores[p, slot] * factor[None]).reshape(BLOCK, wide).astype(BF)
                    parts.append((slot, p, mm(block, cotan[p], 1, 0)))
            for slot, p, part in parts:
                add(listed[slot], p, part)
            return 0

        return step

    done = 0
    for unroll in UNROLLS[pairs]:
        turns = (found - done) // unroll
        lax.fori_loop(0, turns, second(unroll, done), 0)
        done = done + unroll * turns


def near_kernel(root, z_ref, flags, q_ref, k_ref, u_ref, key_all, wide, mine, near, summed, scores, tops, listed):
    rows = q_ref.shape[0]
    per = rows // BLOCK
    z = z_ref[0]
    root = jnp.asarray(root, BF)
    upper, lower = slice(0, rows), slice(rows, 2 * rows)

    @pl.when(z == 0)
    def _():
        near[upper, :] = k_ref[...]

    @pl.when(z == 1)
    def _():
        near[upper, :] = key_all[...]
        near[lower, :] = k_ref[...]

    @pl.when(z < 2)
    def _():
        summed[...] = jnp.zeros_like(summed)

        def query_block(n, _):
            at = rows_of(n)

            def side(p):
                return slice(p * BLOCK, (p + 1) * BLOCK)

            def add(j, p, x):
                summed[rows_of(j), side(p)] += x

            attend(
                n + z * per,
                [split_pair(q_ref[at, side(p)] * root) for p in range(SHARE)],
                [split_pair(u_ref[at, side(p)]) for p in range(SHARE)],
                lambda j, p: near[rows_of(j), side(p)],
                add, flags, scores, tops, listed,
            )
            return 0

        lax.fori_loop(0, per, query_block, 0)

    @pl.when(z == 0)
    def _():
        mine[...] = summed[upper, :]

    @pl.when(z == 1)
    def _():
        wide[...] = summed[upper, :].astype(BF)
        mine[...] = summed[lower, :]


def whole(shape):
    return pl.BlockSpec(shape, lambda i, z, f, n=len(shape): (0,) * n, pipeline_mode=pl.Buffered(1))


def own_columns(rows, chunk):
    return pl.BlockSpec((rows, SHARE * BLOCK), lambda i, z, f: (0, chunk), pipeline_mode=pl.Buffered(1))


def soft_near(here, flags, arrays, key_all, root, chunk):
    rows = arrays[0].shape[0]
    shape = (rows, SHARE * BLOCK)
    blocks = 2 * rows // BLOCK
    return pl.pallas_call(
        functools.partial(near_kernel, root),
        out_shape=[jax.ShapeDtypeStruct(shape, BF), jax.ShapeDtypeStruct(shape, F32)],
        grid_spec=pltpu.PrefetchScalarGridSpec(
            num_scalar_prefetch=2,
            grid=(1,),
            in_specs=[own_columns(rows, chunk)] * 3 + [whole(shape)],
            out_specs=[whole(shape)] * 2,
            scratch_shapes=[
                pltpu.VMEM((2 * rows, SHARE * BLOCK), BF),
                pltpu.VMEM((2 * rows, SHARE * BLOCK), F32),
                pltpu.VMEM((SHARE, blocks, BLOCK // 8, 8, 2 * BLOCK), F32),
                pltpu.VMEM((SHARE, blocks, 8, 2 * BLOCK), F32),
                pltpu.SMEM((blocks + 1,), jnp.int32),
            ],
        ),
        compiler_params=params(),
        cost_estimate=pl.CostEstimate(
            flops=8 * rows * rows * SHARE * BLOCK, transcendentals=2 * rows * rows * SHARE, bytes_accessed=16 * rows * SHARE * BLOCK
        ),
        name="near",
    )(here, flags, *arrays, key_all)


def far_kernel(root, z_ref, flags, q_ref, k_ref, u_ref, key_all, three, key_c, key_d, two_a, two_b, *refs):
    outs, (queries, keys, cotans, summed, scores, tops, listed) = refs[:7], refs[7:]
    three_d, three_e, three_f, out_a, out_b, out_c, mine = outs
    rows = q_ref.shape[0]
    per = rows // BLOCK
    z = z_ref[0]
    root = jnp.asarray(root, BF)

    def part(n):
        return slice(n * rows, (n + 1) * rows)

    def lanes(p):
        return slice(p * BLOCK, (p + 1) * BLOCK)

    def place(n, q, k, u, width):
        queries[part(n), :width] = q * root
        keys[part(2 + n), :width] = k
        cotans[part(n), :width] = u

    def own_of(me):
        pairs = len(OWNED[me])
        return pairs * BLOCK, slice(OWNED[me][0] * BLOCK, (OWNED[me][0] + pairs) * BLOCK)

    for me in range(1, 4):

        @pl.when(z == me)
        def _(me=me):
            width, own = own_of(me)
            if me == 1:
                place(0, two_a[0], two_a[1], two_a[2], width)
                place(1, two_b[0], two_b[1], two_b[2], width)
                keys[part(0), :width] = key_all[:, own]
                keys[part(1), :width] = k_ref[:, own]
            else:
                place(me - 2, q_ref[:, own], k_ref[:, own], u_ref[:, own], width)
                place(3 - me, three[0], three[1], three[2], width)
                keys[part(0), :width] = (key_c if me == 2 else key_d)[...]
                keys[part(1), :width] = (key_d if me == 2 else key_c)[...]

    def far_rows(pairs):
        summed[...] = jnp.zeros_like(summed)

        def query_block(n, _):
            at = rows_of(n)

            def add(j, p, x):
                summed[rows_of(j), lanes(p)] += x

            attend(
                n + 2 * per,
                [split_pair(queries[at, lanes(p)]) for p in range(pairs)],
                [split_pair(cotans[at, lanes(p)]) for p in range(pairs)],
                lambda j, p: keys[rows_of(j), lanes(p)],
                add, flags, scores, tops, listed,
            )
            return 0

        lax.fori_loop(0, 2 * per, query_block, 0)

    @pl.when(z >= 2)
    def _():
        far_rows(3)

    @pl.when(z == 1)
    def _():
        far_rows(2)

    for me in range(1, 4):

        @pl.when(z == me)
        def _(me=me):
            width, _ = own_of(me)
            mine[:, :width] = summed[part(me), :width]
            if me == 1:
                out_c[...] = summed[part(0), :width].astype(BF)
                out_a[...] = summed[part(2), :width].astype(BF)
                out_b[...] = summed[part(3), :width].astype(BF)
            else:
                three_d[...] = summed[part(me - 2), :].astype(BF)
                three_e[...] = summed[part(3 - me), :].astype(BF)
                three_f[...] = summed[part(5 - me), :].astype(BF)


def soft_far(here, flags, arrays, pieces, root, chunk):
    rows = arrays[0].shape[0]
    span = 4 * rows
    shapes = [(rows, 3 * BLOCK)] * 3 + [(rows, 2 * BLOCK)] * 3
    last = (rows, 3 * BLOCK)
    return pl.pallas_call(
        functools.partial(far_kernel, root),
        out_shape=[jax.ShapeDtypeStruct(shape, BF) for shape in shapes] + [jax.ShapeDtypeStruct(last, F32)],
        grid_spec=pltpu.PrefetchScalarGridSpec(
            num_scalar_prefetch=2,
            grid=(1,),
            in_specs=[own_columns(rows, chunk)] * 3 + [whole(piece.shape) for piece in pieces],
            out_specs=[whole(shape) for shape in shapes + [last]],
            scratch_shapes=[
                pltpu.VMEM((2 * rows, 3 * BLOCK), BF),
                pltpu.VMEM((span, 3 * BLOCK), BF),
                pltpu.VMEM((2 * rows, 3 * BLOCK), BF),
                pltpu.VMEM((span, 3 * BLOCK), F32),
                pltpu.VMEM((3, span // BLOCK, BLOCK // 8, 8, 2 * BLOCK), F32),
                pltpu.VMEM((3, span // BLOCK, 8, 2 * BLOCK), F32),
                pltpu.SMEM((span // BLOCK + 1,), jnp.int32),
            ],
        ),
        compiler_params=params(),
        cost_estimate=pl.CostEstimate(
            flops=8 * span * span * BLOCK, transcendentals=2 * span * span, bytes_accessed=64 * span * BLOCK
        ),
        name="far",
    )(here, flags, *arrays, *pieces)


def merge_kernel(z_ref, near, far, wide, three_d, three_e, three_f, two_a, two_b, two_c, lit_ref):
    z = z_ref[0]
    first = slice(0, 2 * BLOCK)
    third, fourth = slice(2 * BLOCK, 5 * BLOCK), slice(5 * BLOCK, 8 * BLOCK)

    @pl.when(z == 0)
    def _():
        for at, x in ((first, two_c), (third, three_d), (fourth, three_e)):
            lit_ref[:, at] = (near[:, at] + wide[:, at].astype(F32) + x[...].astype(F32)).astype(BF)

    @pl.when(z == 1)
    def _():
        lit_ref[:, first] = (near[:, first] + far[:, first]).astype(BF)
        lit_ref[:, third] = (near[:, third] + three_e[...].astype(F32)).astype(BF)
        lit_ref[:, fourth] = (near[:, fourth] + three_d[...].astype(F32)).astype(BF)

    @pl.when(z == 2)
    def _():
        lit_ref[:, first] = two_a[...]
        lit_ref[:, third] = far[...].astype(BF)
        lit_ref[:, fourth] = three_f[...]

    @pl.when(z == 3)
    def _():
        lit_ref[:, first] = two_b[...]
        lit_ref[:, third] = three_f[...]
        lit_ref[:, fourth] = far[...].astype(BF)


def merge(here, near, far, wide, pieces):
    vmem = pl.BlockSpec(memory_space=pltpu.VMEM)
    return pl.pallas_call(
        merge_kernel,
        out_shape=jax.ShapeDtypeStruct(near.shape, BF),
        in_specs=[pl.BlockSpec(memory_space=pltpu.SMEM)] + [vmem] * 9,
        out_specs=vmem,
        compiler_params=params(24),
        cost_estimate=pl.CostEstimate(flops=4 * near.size, transcendentals=0, bytes_accessed=10 * near.size),
        name="merge",
    )(here, near, far, wide, *pieces)


def triangle():
    row = lax.broadcasted_iota(jnp.int32, (BLOCK, BLOCK), 0)
    column = lax.broadcasted_iota(jnp.int32, (BLOCK, BLOCK), 1)
    return row >= column


def spread_decays(decays, first, width, each):
    heads = decays.shape[1]
    head = lax.broadcasted_iota(jnp.int32, (heads, width), 0)
    lane = lax.broadcasted_iota(jnp.int32, (heads, width), 1)
    spread = (head == first + lane // each).astype(F32).astype(BF)
    return mm(decays, spread, 1, 0).astype(BF)


def device_levels(decays, first, width):
    wide = spread_decays(decays, first, width, BLOCK // 2)
    lower = triangle().astype(F32).astype(BF)
    before = jnp.zeros((1, width), F32)
    levels = []
    for b in range(decays.shape[0] // BLOCK):
        level = mm(lower, wide[b * BLOCK : (b + 1) * BLOCK], 1, 0)
        levels.append(level + before)
        before = before + level[BLOCK - 1 :]
    return jnp.concatenate(levels, axis=0), before


def by_lane(first, second):
    lane = lax.broadcasted_iota(jnp.int32, first.shape, 1)
    return jnp.where(lane < BLOCK // 2, first, second)


def on_diagonal(x):
    row = lax.broadcasted_iota(jnp.int32, x.shape, 0)
    lane = lax.broadcasted_iota(jnp.int32, x.shape, 1)
    half = BLOCK // 2
    return jnp.where((row < half) == (lane < half), x, 0.0)


def fold(x):
    return x[: BLOCK // 2] + x[BLOCK // 2 :]


def state_kernel(q_ref, k_ref, v_ref, d_ref, sum_ref, total_ref, scaled_ref):
    level, last = device_levels(d_ref[...], 2 * pl.program_id(0), BLOCK)
    key = (k_ref[...].astype(F32) * jnp.exp(level - last)).astype(BF)
    sum_ref[0] = fold(on_diagonal(mm(key, v_ref[...], 0, 0))).astype(BF)
    thirds, rest = [], last
    for _ in range(3):
        thirds.append(rest.astype(BF))
        rest = rest - thirds[-1].astype(F32)
    blank = jnp.zeros((total_ref.shape[1] - 3, BLOCK), BF)
    total_ref[0] = jnp.concatenate(thirds + [blank], axis=0)
    scaled_ref[...] = (q_ref[...].astype(F32) * jnp.exp(-level)).astype(BF)


def device_state(light_query, light_key, light_value, decays, pairs):
    rows = light_key.shape[0]
    block = pl.BlockSpec((rows, BLOCK), lambda p: (0, p))
    return pl.pallas_call(
        state_kernel,
        out_shape=[
            jax.ShapeDtypeStruct((pairs, BLOCK // 2, BLOCK), BF),
            jax.ShapeDtypeStruct((pairs, 8, BLOCK), BF),
            jax.ShapeDtypeStruct(light_query.shape, BF),
        ],
        grid=(pairs,),
        in_specs=[block, block, block, pl.BlockSpec(decays.shape, lambda p: (0, 0))],
        out_specs=[
            pl.BlockSpec((1, BLOCK // 2, BLOCK), lambda p: (p, 0, 0)),
            pl.BlockSpec((1, 8, BLOCK), lambda p: (p, 0, 0)),
            block,
        ],
        compiler_params=params(60),
        cost_estimate=pl.CostEstimate(
            flops=8 * rows * pairs * BLOCK * BLOCK, transcendentals=rows * pairs * BLOCK, bytes_accessed=8 * rows * pairs * BLOCK
        ),
        name="state",
    )(light_query, light_key, light_value, decays)


def take_lit(count, z, lits, held):
    @pl.when(pl.program_id(0) == 0)
    def _():
        per = lits[0].shape[1] // BLOCK
        for k in range(count):
            owner = lax.rem(z - k + count, count)
            for p in range(per):
                held[owner * per + p] = lits[k][:, p * BLOCK : (p + 1) * BLOCK]


def reach_kernel(count, z_ref, q_ref, *refs):
    lits, sum_ref = refs[:count], refs[count]
    _, width = lits[0].shape
    per = width // BLOCK
    for k in range(count):
        owner = lax.rem(z_ref[0] - k + count, count)
        for p in range(per):
            at = pl.ds(pl.multiple_of((owner * per + p) * BLOCK, BLOCK), BLOCK)
            product = mm(q_ref[:, at], lits[k][:, p * BLOCK : (p + 1) * BLOCK], 0, 0)
            sum_ref[owner * per + p] = fold(on_diagonal(product)).astype(BF)


def device_reach(here, scaled, lits, chunk):
    count = len(lits)
    rows, width = lits[0].shape
    pairs = count * width // BLOCK
    return pl.pallas_call(
        functools.partial(reach_kernel, count),
        out_shape=jax.ShapeDtypeStruct((pairs, BLOCK // 2, BLOCK), BF),
        grid_spec=pltpu.PrefetchScalarGridSpec(
            num_scalar_prefetch=1,
            grid=(1,),
            in_specs=[pl.BlockSpec((rows, count * width), lambda p, z: (0, chunk))]
            + [pl.BlockSpec((rows, width), lambda p, z: (0, 0))] * count,
            out_specs=pl.BlockSpec((pairs, BLOCK // 2, BLOCK), lambda p, z: (0, 0, 0)),
        ),
        compiler_params=params(),
        cost_estimate=pl.CostEstimate(
            flops=2 * rows * pairs * BLOCK * BLOCK, transcendentals=0, bytes_accessed=4 * rows * pairs * BLOCK
        ),
        name="reach",
    )(here, scaled, *lits)


def chain_kernel(x_ref, a_ref, o_ref):
    count, half = x_ref.shape[0], x_ref.shape[1] // 2
    zero = jnp.zeros((half, x_ref.shape[2]), F32)

    def step(n, carried):
        early, late = carried
        m = count - 1 - n
        o_ref[n, :half, :] = early.astype(BF)
        o_ref[m, half:, :] = late.astype(BF)
        early = a_ref[n] * early + x_ref[n, :half, :].astype(F32)
        late = a_ref[m] * late + x_ref[m, half:, :].astype(F32)
        return early, late

    lax.fori_loop(0, count, step, (zero, zero))


def chain(items, totals):
    vmem = pl.BlockSpec(memory_space=pltpu.VMEM)
    return pl.pallas_call(
        chain_kernel,
        out_shape=jax.ShapeDtypeStruct(items.shape, BF),
        in_specs=[vmem, vmem],
        out_specs=vmem,
        compiler_params=params(),
        cost_estimate=pl.CostEstimate(flops=2 * items.size, transcendentals=0, bytes_accessed=8 * items.size),
        name="chain",
    )(items, totals)


def local_kernel(count, first_pair, skip, olds, scale, z_ref, q_ref, k_ref, v_ref, d_ref, *refs):
    lits = refs[:count]
    gq_ref, gk_ref, gv_ref, lit_ref, held = refs[count + olds :]
    take_lit(count, z_ref[0], lits, held)
    here = pl.program_id(0)
    blocks = q_ref.shape[0] // BLOCK
    shape = (BLOCK, BLOCK)
    row_at = lax.broadcasted_iota(jnp.int32, shape, 0)
    lane_at = lax.broadcasted_iota(jnp.int32, shape, 1)
    lower, upper = row_at >= lane_at, row_at <= lane_at
    ones_lower, ones_upper = (side.astype(F32).astype(BF) for side in (lower, upper))
    slot = skip + here
    spread = spread_decays(d_ref[...], 2 * (first_pair + slot), 2 * BLOCK, BLOCK)
    heads = d_ref.shape[1]
    picked = lax.broadcasted_iota(jnp.int32, (8, heads), 1) - 2 * (first_pair + slot)
    picked = picked == lax.broadcasted_iota(jnp.int32, (8, heads), 0) // 4
    lines = mm(picked.astype(F32).astype(BF), d_ref[...], 1, 1).astype(BF)
    lit_ref[...] = held[slot]
    state = None
    kept = []
    for b in range(blocks):
        at = slice(b * BLOCK, (b + 1) * BLOCK)
        query, key, value, lit = (q_ref[at, :], k_ref[at, :], v_ref[at, :], held[slot, at, :])
        levels = mm(ones_lower, spread[at], 1, 0)
        lined = mm(lines[:, at], ones_upper, 1, 0)
        columns = (levels[:, :BLOCK], levels[:, BLOCK:])
        level = by_lane(*columns)
        last = level[BLOCK - 1 :]
        entries = jnp.exp(-level)
        leaving = jnp.exp(level - last)
        decay = jnp.exp(-last)
        spans = [lined[4 * n : 4 * n + 1] - columns[n] for n in range(2)]
        weights = jnp.concatenate(
            [jnp.where(lower, jnp.exp(jnp.minimum(span, 0.0)), 0.0) for span in spans], axis=1
        )
        turned = jnp.concatenate(
            [jnp.where(upper, jnp.exp(jnp.minimum(-span, 0.0)), 0.0) for span in spans], axis=1
        )
        queries, keys, values, twice = (split_pair(query), split_pair(key), split_pair(value), split_pair(lit))
        back = (mm(lit, values, 1, 1) * weights).astype(BF)
        back_turned = (mm(value, twice, 1, 1) * turned).astype(BF)
        mixed_turned = (mm(key, queries, 1, 1) * turned).astype(BF)
        grad_query = mm(back, keys, 1, 0)
        if state is not None:
            grad_query = grad_query + entries * mm(lit, state.astype(BF), 1, 1)
        gq_ref[at, :] = scale * grad_query
        grad_key = mm(back_turned, queries, 1, 0)
        grad_value = mm(mixed_turned, twice, 1, 0)
        kept.append((grad_key, grad_value, entries, leaving, decay))
        if b < blocks - 1:
            left = (key.astype(F32) * leaving).astype(BF)
            left = on_diagonal(mm(left, value, 0, 0))
            state = left if state is None else decay * state + left
    state = None
    for b in reversed(range(blocks)):
        at = slice(b * BLOCK, (b + 1) * BLOCK)
        grad_key, grad_value, entries, leaving, decay = kept[b]
        if state is not None:
            low = state.astype(BF)
            grad_key = grad_key + leaving * mm(v_ref[at, :], low, 1, 1)
            grad_value = grad_value + leaving * mm(k_ref[at, :], low, 1, 0)
        gk_ref[at, :] = scale * grad_key
        gv_ref[at, :] = scale * grad_value
        if b > 0:
            query = (q_ref[at, :].astype(F32) * entries).astype(BF)
            query = on_diagonal(mm(query, held[slot, at, :], 0, 0))
            state = query if state is None else decay * state + query


def local(here, light_query, light_key, light_value, decays, lits, first, skip, many, olds, scale):
    count = len(lits)
    rows, columns = light_query.shape
    width = lits[0].shape[1]
    pairs = count * width // BLOCK
    block = pl.BlockSpec((rows, BLOCK), lambda p, z: (0, first + skip + p))
    base = 5 + count
    return pl.pallas_call(
        functools.partial(local_kernel, count, first, skip, len(olds), scale),
        out_shape=[jax.ShapeDtypeStruct((rows, columns), F32)] * 3 + [jax.ShapeDtypeStruct((rows, columns), BF)],
        grid_spec=pltpu.PrefetchScalarGridSpec(
            num_scalar_prefetch=1,
            grid=(many,),
            in_specs=[
                block,
                block,
                block,
                pl.BlockSpec(decays.shape, lambda p, z: (0, 0)),
            ]
            + [pl.BlockSpec((rows, width), lambda p, z: (0, 0))] * count
            + [pl.BlockSpec(memory_space=pl.ANY)] * len(olds),
            out_specs=[block] * 4,
            scratch_shapes=[pltpu.VMEM((pairs, rows, BLOCK), BF)],
        ),
        input_output_aliases={base + n: n for n in range(len(olds))},
        compiler_params=params(60),
        cost_estimate=pl.CostEstimate(
            flops=40 * rows * many * BLOCK * BLOCK, transcendentals=4 * rows * many * BLOCK, bytes_accessed=22 * rows * many * BLOCK
        ),
        name="local",
    )(here, light_query, light_key, light_value, decays, *lits, *olds)


def wide_state(x):
    pairs = x.shape[0]
    width = pairs * BLOCK
    x = jnp.concatenate([x[p] for p in range(pairs)], axis=1)
    x = jnp.concatenate([x] * (2 * pairs), axis=0)
    half = BLOCK // 2
    row = lax.broadcasted_iota(jnp.int32, (width, width), 0) // half
    lane = lax.broadcasted_iota(jnp.int32, (width, width), 1) // half
    return x * (row == lane).astype(F32).astype(BF)


def final_kernel(scale, pq_ref, pk_ref, pv_ref, lit_ref, k_ref, v_ref, d_ref, s_ref, r_ref, gq_ref, gk_ref, gv_ref):
    pairs = s_ref.shape[0]
    width = pairs * BLOCK
    level, last = device_levels(d_ref[...], 2 * pairs * pl.program_id(0), width)
    entries = scale * jnp.exp(-level)
    leaving = scale * jnp.exp(level - last)
    state, reach = wide_state(s_ref[...]), wide_state(r_ref[...])
    gq_ref[...] = (pq_ref[...] + entries * mm(lit_ref[...], state, 1, 1)).astype(BF)
    gk_ref[...] = (pk_ref[...] + leaving * mm(v_ref[...], reach, 1, 1)).astype(BF)
    gv_ref[...] = (pv_ref[...] + leaving * mm(k_ref[...], reach, 1, 0)).astype(BF)


def final(parts, light_key, light_value, decays, state_in, reach_in, scale):
    rows, columns = light_key.shape
    pairs = columns // BLOCK
    step = 2 if pairs % 2 == 0 else 1
    block = pl.BlockSpec((rows, step * BLOCK), lambda p: (0, p))
    small = pl.BlockSpec((step, BLOCK // 2, BLOCK), lambda p: (p, 0, 0))
    return pl.pallas_call(
        functools.partial(final_kernel, scale),
        out_shape=[jax.ShapeDtypeStruct((rows, columns), BF)] * 3,
        grid=(pairs // step,),
        in_specs=[block] * 6 + [pl.BlockSpec(decays.shape, lambda p: (0, 0)), small, small],
        out_specs=[block] * 3,
        compiler_params=params(60),
        cost_estimate=pl.CostEstimate(
            flops=6 * rows * columns * BLOCK, transcendentals=2 * rows * columns, bytes_accessed=24 * rows * columns
        ),
        name="final",
    )(*parts, light_key, light_value, decays, state_in, reach_in)


def turn(pieces, count):
    return [pieces[0]] + [
        lax.ppermute(pieces[k], "head", [(i, (i + k) % count) for i in range(count)])
        for k in range(1, count)
    ]


def program(light_query, light_key, light_value, soft_query, soft_key, upstream, decays, block_mask):
    count, spans = lax.axis_size("head"), lax.axis_size("ctx")
    devices = count * spans
    _, columns = light_query.shape
    heads = decays.shape[1]
    head_width = columns // heads
    pairs = heads // 2
    share = pairs // count
    chunks = 2 if share % 2 == 0 else 1
    per = share // chunks
    assert 2 * head_width == BLOCK and share * count == pairs
    part = count * per * head_width // devices
    again = head_width // part
    assert part * again == head_width
    scale = 1.0 / (head_width * math.sqrt(head_width))
    root = 1.0 / math.sqrt(head_width)
    here = lax.axis_index("head").astype(jnp.int32).reshape(1)

    arrays = (soft_query, soft_key, upstream)
    quad = count == 4 and chunks * SHARE == pairs
    packed = []
    for c in range(chunks):
        if quad:
            pieces = pack_quad(here, arrays, c)
        else:
            pieces = pack(here, arrays, c, count, per * BLOCK)
        packed.append(turn_in(pieces) if quad else turn(pieces, count))
    near, wide = [], []
    if quad:
        for c in range(chunks):
            sent, kept = soft_near(here, block_mask, arrays, packed[c][0], root, c)
            near.append(kept)
            wide.append(send(sent, (1, 0)))
    sums, totals, scaled = device_state(light_query, light_key, light_value, decays, pairs)

    parts, reaches = (), []
    for c in range(chunks):
        if quad:
            *lits, far = soft_far(here, block_mask, arrays, packed[c], root, c)
        else:
            lits = soft(here, block_mask, packed[c], root)
        lits = turn_out(lits) if quad else turn(lits, count)
        if quad:
            lits = (merge(here, near[c], far, wide[c], lits),)
        reaches.append(device_reach(here, scaled, lits, c))
        first, many = c * count * per, count * per
        cuts = (0, many // 2, many) if c == chunks - 1 else (0, many)
        for n in range(len(cuts) - 1):
            parts = local(
                here, light_query, light_key, light_value, decays, lits, first,
                cuts[n], cuts[n + 1] - cuts[n], tuple(parts), scale,
            )

    def exchange(x):
        return lax.all_to_all(x, AXES, split_axis=0, concat_axis=0, tiled=True)

    def spread(x):
        x = x.reshape(chunks, devices, part, BLOCK)
        return jnp.swapaxes(x, 0, 1).reshape(devices, chunks * part, BLOCK)

    def gather(x):
        x = x.reshape(devices, chunks, part, BLOCK)
        return jnp.swapaxes(x, 0, 1).reshape(pairs, head_width, BLOCK)

    thirds = jnp.transpose(totals[:, :3].reshape(chunks, count * per, 3, BLOCK), (1, 2, 0, 3))
    thirds = jnp.repeat(thirds.reshape(count * per, 3 * chunks, BLOCK), again, axis=0)
    half = chunks * part
    fill = jnp.zeros((devices, -(2 * half + 3 * chunks) % 8, BLOCK), BF)
    sends = [spread(sums), spread(jnp.concatenate(reaches, axis=0)), thirds, fill]
    got = exchange(jnp.concatenate(sends, axis=1))
    thirds = got[:, 2 * half : 2 * half + 3 * chunks].astype(F32).reshape(devices, 3, chunks, BLOCK)
    rates = jnp.exp(-(thirds[:, 0] + thirds[:, 1] + thirds[:, 2]))
    rates = jnp.repeat(rates, part, axis=1)
    given = chain(got[:, : 2 * half], rates)
    given = exchange(given)
    return tuple(
        final(parts, light_key, light_value, decays, gather(given[:, :half]), gather(given[:, half:]), scale)
    )


def solution(mesh):
    rows = P(AXES, None)
    return jax.shard_map(
        program,
        mesh=mesh,
        in_specs=(rows,) * 7 + (P("ctx", None),),
        out_specs=(rows,) * 3,
        check_vma=False,
    )
```
